256 devices in a mesh: stripe: 8 (over y, x_hi), scan: 32 (over z, x_lo, core).
Axes of the slice: x: 4 (x_hi: 2, x_lo: 2; x = x_hi * 2 + x_lo), y: 4, z: 8, core: 2. Of those that a mesh axis runs over, the one named last changes fastest.
Arguments:
- dose: bfloat16 [1600, 3200], P('stripe', 'scan'), may hold values from 0 to 4
- target: int32 [1600, 3200], P('stripe', 'scan'), may hold values 0 or 1
- psf: bfloat16 [61, 61], replicated, may hold values from 0 to 0.025
Outputs:
- resist: float32 [1600, 3200], P('stripe', 'scan')
- dose_out: float32 [1600, 3200], P('stripe', 'scan')
The draws below stay inside these ranges and needn't reach their ends.
All inputs are finite; a program needn't handle non-finite values. No bound on the sum of `target` on one device may be relied on, other than what follows from the above.
Results may differ from the reference program's by a relative error of at most 0.0003.
Values may be sent and summed in bfloat16 or wider, within the bound.
A program may use at most 64 MiB of HBM per device.

```python
import math
import jax
import jax.numpy as jnp
from jax import lax

TX = 200
TY = 100
TAPS = 61
COARSE = 25
SIGMA = 40
ITERS = 4
RIM = 30
NX = 1600
NY = 3200
NCX = 64
NCY = 128


def draw_dose(key, part):
    first, second, third = jax.random.split(key, 3)
    tile_bits = jax.random.randint(first, (NX // TX, NY // TY), 0, 2)
    tile_level = 0.15 + 1.75 * tile_bits.astype(jnp.float32)
    cell_level = jnp.exp(jax.random.uniform(second, (NX // COARSE, NY // COARSE), jnp.float32, math.log(0.6), math.log(1.0)))
    fine = jnp.clip(1.0 + 0.4 * jax.random.normal(third, (NX, NY), jnp.float32), 0.0, 2.0)
    tiles = jnp.repeat(jnp.repeat(tile_level, TX, axis=0), TY, axis=1)
    cells = jnp.repeat(jnp.repeat(cell_level, COARSE, axis=0), COARSE, axis=1)
    return (tiles * cells * fine).astype(jnp.bfloat16)


def draw_psf(key, part):
    offsets = (jnp.arange(TAPS, dtype=jnp.int32) - (TAPS - 1) // 2).astype(jnp.float32)
    radius_sq = offsets[:, None] * offsets[:, None] + offsets[None, :] * offsets[None, :]
    radius = jnp.sqrt(radius_sq)
    factor = jax.random.uniform(key, (TAPS, TAPS), jnp.float32, 0.5, 1.5)
    shape_core = 0.7 * jnp.exp(-radius_sq / 18.0) / 56.5
    shape_tail = 0.3 * jnp.exp(-radius / 12.0) / 905.0
    return (factor * (shape_core + shape_tail)).astype(jnp.bfloat16)


def with_ends(entries, own_key, low, largest):
    index_at = [jax.random.randint(jax.random.fold_in(own_key, axis), (), 0, length) for axis, length in enumerate(entries.shape)]
    main_axis = entries.shape.index(max(entries.shape))
    beside = index_at[:main_axis] + [(index_at[main_axis] + 1) % entries.shape[main_axis]] + index_at[main_axis + 1:]
    return entries.at[tuple(index_at)].set(low).at[tuple(beside)].set(largest)


def setup_inputs(seed: int = 0) -> dict:
    arg_keys = jax.random.split(jax.random.key(seed), 4)
    dose = draw_dose(jax.random.fold_in(arg_keys[3], 71), 0)
    target = with_ends((jax.random.randint(arg_keys[1], (NX, NY), 0, 2) < 1).astype(jnp.int32), jax.random.fold_in(arg_keys[1], 1), 0, 1)
    psf = draw_psf(jax.random.fold_in(arg_keys[3], 71), 0)
    return {"dose": dose, "target": target, "psf": psf}


back_ratio = 0.6
resist_gain = 3.0
resist_level = 1.5
step_length = 0.5

def gauss_table(count):
    index = jnp.arange(count, dtype=jnp.int32)
    dist = (index[:, None] - index[None, :]).astype(jnp.float32)
    return jnp.exp(-dist * dist / (2.0 * SIGMA * SIGMA)) / (math.sqrt(2.0 * math.pi) * SIGMA)

def correlate(field, kern):
    size_a = NX + 4 * RIM
    size_b = NY + 4 * RIM
    padded = jnp.pad(field, RIM)
    spec = jnp.fft.rfft2(padded, s=(size_a, size_b)) * jnp.fft.rfft2(kern[::-1, ::-1], s=(size_a, size_b))
    full = jnp.fft.irfft2(spec, s=(size_a, size_b))
    return full[2 * RIM:2 * RIM + NX, 2 * RIM:2 * RIM + NY].astype(jnp.float32)

def upsample(cells):
    return jnp.repeat(jnp.repeat(cells, COARSE, axis=0), COARSE, axis=1)

def reference(dose, target, psf):
    kern = psf.astype(jnp.float32)
    mask = target.astype(jnp.float32)
    table_rows = gauss_table(NCX)
    table_cols = gauss_table(NCY)
    hi = lax.Precision.HIGHEST
    current = dose
    resist = jnp.zeros((NX, NY), jnp.float32)
    updated = jnp.zeros((NX, NY), jnp.float32)
    for step in range(ITERS):
        field = lax.optimization_barrier(current).astype(jnp.float32)
        blurred = correlate(field, kern)
        cells = field.reshape(NCX, COARSE, NCY, COARSE).mean(axis=(1, 3))
        back = jnp.dot(jnp.dot(table_rows, cells, precision=hi), table_cols, precision=hi)
        exposure = blurred + back_ratio * upsample(back)
        resist = jax.nn.sigmoid(resist_gain * (exposure - resist_level))
        error = (resist - mask) * resist_gain * resist * (1.0 - resist)
        error_half = lax.optimization_barrier(error.astype(jnp.bfloat16)).astype(jnp.float32)
        adjoint = correlate(error_half, kern[::-1, ::-1])
        sums = error.reshape(NCX, COARSE, NCY, COARSE).sum(axis=(1, 3))
        back_adjoint = jnp.dot(jnp.dot(table_rows, sums, precision=hi), table_cols, precision=hi)
        gradient = adjoint + back_ratio / (COARSE * COARSE) * upsample(back_adjoint)
        updated = field - step_length * gradient
        current = updated.astype(jnp.bfloat16)
    return (resist, updated)
```

```python
import math

import jax
import jax.numpy as jnp
from jax import lax
from jax.experimental import pallas as pl
from jax.experimental.pallas import tpu as pltpu
from jax.sharding import PartitionSpec as P

TX, TY = 200, 100
TAPS = 61
COARSE = 25
SIGMA = 40
ITERS = 4
RIM = 30
BACK = 0.6
GAIN = 3.0
LEVEL = 1.5
STEP = 0.5
CROW, CCOL = TX // COARSE, TY // COARSE
ADJ_SCALE = BACK / (COARSE * COARSE)

MESH = pl.DeviceIdType.MESH
F32, BF16 = jnp.float32, jnp.bfloat16
HI = lax.Precision.HIGHEST

EROWS = 336
CROWS = 272
AOUT = 264
AIN = 320
BIN = 256
PHASES = ITERS + 1
SIDE = 208
EDGE = 64
HALO = 2 * SIDE + 6 * EDGE


def iota(shape, dim):
    return lax.broadcasted_iota(jnp.int32, shape, dim)


def dot(a, b, precision=None):
    return jnp.dot(a, b, precision=precision, preferred_element_type=F32)


def dot_nt(a, b, precision=None):
    return lax.dot_general(
        a, b, (((1,), (1,)), ((), ())), precision=precision, preferred_element_type=F32
    )


def gauss(dist):
    d = dist.astype(F32)
    return jnp.exp(-d * d / (2.0 * SIGMA * SIGMA)) / (math.sqrt(2.0 * math.pi) * SIGMA)


def cell_of(col):
    out = jnp.full(col.shape, -3, jnp.int32)
    for k in range(-2, 7):
        out = out + jnp.where(col >= COARSE * k, 1, 0)
    return out


def kernel(
    ns, nn, dose_ref, target_ref, psf_ref, resist_ref, updated_ref,
    g1, g2, halo, tile, bottom, et0, et1, ct0, ct1, at0, at1, wa, wf, vv,
    ps, rf, ra, fr, xa, xb, err, own, zs, sc, m1, cu, ub0, ub1, bk,
    send_sem, recv_sem,
):
    s = lax.axis_index("stripe")
    n = lax.axis_index("scan")
    ncx, ncy = ns * CROW, nn * CCOL
    up, down = lax.rem(s + ns - 1, ns), lax.rem(s + 1, ns)
    left, right = lax.rem(n + nn - 1, nn), lax.rem(n + 1, nn)

    barrier = pltpu.get_barrier_semaphore()

    def hello(a, b):
        pl.semaphore_signal(barrier, inc=1, device_id=(a, b), device_id_type=MESH)

    for k in range(1, ns):
        hello(lax.rem(s + k, ns), n)
    for k in range(1, nn):
        hello(s, lax.rem(n + k, nn))
    for a in (up, down):
        for b in (left, right):
            hello(a, b)

    lane = iota((1, 128), 1)

    def field_out(value):
        tile[0:TX, :] = value.astype(BF16)
        bottom[...] = value[TX - EDGE:, :].astype(BF16)

    def col_sum(ref):
        total = ref[pl.ds(0, CROW, stride=COARSE), :]
        for u in range(1, COARSE):
            total = total + ref[pl.ds(u, CROW, stride=COARSE), :]
        return total

    pick = jnp.where(cell_of(iota((16, 128), 1)) == iota((16, 128), 0), 1.0, 0.0)
    pick = jnp.where((iota((16, 128), 0) < CCOL) & (iota((16, 128), 1) < TY), pick, 0.0)
    pick2 = jnp.where(cell_of(iota((16, 128), 1)) == iota((16, 128), 0) - 10, 1.0, 0.0)
    pick2 = jnp.where(
        (iota((16, 128), 0) >= 8) & (iota((16, 128), 1) < TY)
        & (iota((16, 128), 0) < 10 + CCOL) & (iota((16, 128), 0) >= 10), pick2, 0.0)
    picks = pick + pick2

    zs[...] = jnp.zeros_like(zs)
    sc[...] = jnp.zeros_like(sc)

    def payload(err_cols, cur_cols, spread):
        both = dot_nt(picks, jnp.concatenate([err_cols, cur_cols], axis=0), HI)
        sc[:, 0:16] = both
        first = jnp.where(lane < CROW, sc[0:8, :], 0.0)
        second = jnp.where((lane >= 8) & (lane < 16), sc[8:16, :], 0.0)
        sums = pltpu.roll(first, s * CROW, 1)
        cells = pltpu.roll(second, 64 - 8 + s * CROW, 1) * (1.0 / (COARSE * COARSE))
        if spread is not None:
            zs[:, 0:8] = spread
            part = jnp.zeros((8, 128), F32)
            for d in range(5):
                part = part + pltpu.roll(zs[8 * d:8 * d + 8, :], 62 + d + s * CROW, 1)
            cells = cells - (STEP / (COARSE * COARSE)) * part
        return jnp.where(lane < 64, sums, cells)

    def start_global1(t, value):
        g1[t, s] = value
        for k in range(1, ns):
            pltpu.make_async_remote_copy(
                g1.at[t, s], g1.at[t, s], send_sem.at[0], recv_sem.at[t, 0],
                device_id=(lax.rem(s + k, ns), n), device_id_type=MESH,
            ).start()

    def start_global2(t, value):
        g2[t, n] = value
        for k in range(1, nn):
            pltpu.make_async_remote_copy(
                g2.at[t, n], g2.at[t, n], send_sem.at[1], recv_sem.at[t, 1],
                device_id=(s, lax.rem(n + k, nn)), device_id_type=MESH,
            ).start()

    def start_halo(t):
        def go(src, first, rows, a, b):
            pltpu.make_async_remote_copy(
                src, halo.at[t, pl.ds(first, rows)], send_sem.at[2], recv_sem.at[t, 2],
                device_id=(a, b), device_id_type=MESH,
            ).start()

        top = tile.at[pl.ds(0, EDGE)]
        first = 2 * SIDE
        go(tile, 0, SIDE, s, right)
        go(tile, SIDE, SIDE, s, left)
        go(bottom, first, EDGE, down, n)
        go(top, first + EDGE, EDGE, up, n)
        go(bottom, first + 2 * EDGE, EDGE, down, right)
        go(bottom, first + 3 * EDGE, EDGE, down, left)
        go(top, first + 4 * EDGE, EDGE, up, right)
        go(top, first + 5 * EDGE, EDGE, up, left)

    def all_of(ref, sem_send, sem_recv):
        return pltpu.make_async_remote_copy(
            ref, ref, sem_send, sem_recv, device_id=(s, right), device_id_type=MESH
        )

    def of_global1(t):
        return all_of(g1.at[t, pl.ds(0, ns - 1)], send_sem.at[0], recv_sem.at[t, 0])

    def of_global2(t):
        return all_of(g2.at[t, pl.ds(0, nn - 1)], send_sem.at[1], recv_sem.at[t, 1])

    def of_halo(t):
        return all_of(halo.at[t], send_sem.at[2], recv_sem.at[t, 2])

    def assemble(t, centre):
        yes = lambda c: jnp.where(c, 1.0, 0.0).astype(F32)
        has_up, has_down = yes(s > 0), yes(s < ns - 1)
        has_left, has_right = yes(n > 0), yes(n < nn - 1)
        first = 2 * SIDE

        def band(row, rows, mid, lhs, rhs, flag):
            lhs = pltpu.roll(lhs, 28, 1) * (has_left * flag)
            rhs = pltpu.roll(rhs, TY, 1) * (has_right * flag)
            et0[row:row + rows, :] = jnp.where(lane < TY, mid * flag, rhs)
            et1[row:row + rows, :] = jnp.where(lane < 32, rhs, jnp.where(lane >= 68, lhs, 0.0))

        def part(k, rows):
            return halo[t, pl.ds(k, rows), :].astype(F32)

        band(0, EDGE, part(first, EDGE), part(first + 2 * EDGE, EDGE), part(first + 3 * EDGE, EDGE), has_up)
        band(EDGE, TX, centre, part(0, TX), part(SIDE, TX), jnp.float32(1.0))
        band(EDGE + TX, EDGE, part(first + EDGE, EDGE), part(first + 4 * EDGE, EDGE), part(first + 5 * EDGE, EDGE), has_down)

    def global1_result(t):
        total = g1[t, 0]
        for k in range(1, ns):
            total = total + g1[t, k]
        return dot(total, m1[...], HI)

    def global2_result(t):
        stack = g2[t].reshape(nn * 8, 128)
        turned = jnp.transpose(stack)[0:32, :]
        return dot(turned, cu[...], HI)

    def set_back(out):
        value = BACK * (out[16:24, 256:384] + out[24:32, 384:512])
        for u in range(COARSE):
            bk[pl.ds(u, CROW, stride=COARSE), :] = value

    ps[...] = jnp.zeros_like(ps)
    ps[0:TAPS, 0:TAPS] = psf_ref[...].astype(F32)
    taps = ps[...]
    taps_h = taps.astype(BF16)
    b_at, l_at = iota((128, 128), 0), iota((128, 128), 1)
    perm_f = jnp.where((l_at == lax.rem(RIM - b_at + 256, 128)) & (b_at < TAPS), 1.0, 0.0).astype(BF16)
    perm_a = jnp.where((l_at == lax.rem(b_at - RIM + 256, 128)) & (b_at < TAPS), 1.0, 0.0).astype(BF16)
    flip = jnp.where(iota((64, 64), 1) == TAPS - 1 - iota((64, 64), 0), 1.0, 0.0).astype(BF16)
    rf[...] = dot(taps_h, perm_f)
    ra[...] = dot(dot(flip, taps_h).astype(BF16), perm_a)

    dose = jnp.zeros((TX, 128), F32)
    own[...] = dose
    own[:, 0:TY] = dose_ref[...].astype(F32)
    tile[...] = jnp.zeros_like(tile)
    field_out(own[...])
    first_payload = payload(jnp.zeros((8, 128), F32), col_sum(own), None)

    g_row = jnp.bitwise_and(b_at, 63)
    full_rows = gauss(iota((ncx, ncx), 0) - iota((ncx, ncx), 1))
    twice = dot(full_rows, gauss(iota((ncx, 128), 0) - (s * CROW + iota((ncx, 128), 1) - 16)), HI)
    upper = jnp.concatenate([twice, jnp.zeros((128 - ncx, 128), F32)], axis=0)
    low = b_at < 64
    table = jnp.where(low & (l_at < 12), gauss(g_row - (s * CROW + l_at - 2)), 0.0)
    table = table + jnp.where(low & (l_at >= 16) & (l_at < 24), upper, 0.0)
    table = table + jnp.where((~low) & (l_at >= 24) & (l_at < 32), gauss(g_row - (s * CROW + l_at - 24)), 0.0)
    table = jnp.where(g_row < ncx, table, 0.0)
    m1[...] = table

    pl.semaphore_wait(barrier, ns - 1 + nn - 1 + 4)
    start_global1(0, first_payload)
    start_halo(0)

    rows8 = nn * 8
    q = jnp.bitwise_and(iota((rows8, 256), 0), 7)
    dev = iota((rows8, 256), 0) // 8
    pos = iota((rows8, 256), 1)
    col = jnp.where(pos < 160, pos, pos - 256)
    cu[:, 0:256] = jnp.where(q < CCOL, gauss(CCOL * dev + q - (CCOL * n + cell_of(col))), 0.0)
    q1, dev1 = q[:, 0:128], dev[:, 0:128]
    lane_cell = CCOL * n + cell_of(iota((rows8, 128), 1))
    mid_at = iota((ncy, 128), 0)
    mid = gauss(mid_at - (CCOL * n + cell_of(iota((ncy, 128), 1))))
    qf = jnp.bitwise_and(iota((rows8, ncy), 0), 7)
    outer = jnp.where(qf < CCOL, gauss(CCOL * (iota((rows8, ncy), 0) // 8) + qf - iota((rows8, ncy), 1)), 0.0)
    cu[:, 256:384] = (-STEP * ADJ_SCALE) * dot(outer, mid, HI)
    at = CCOL * dev1 + q1 - 2
    cu[:, 384:512] = jnp.where((at >= 0) & (at < ncy), gauss(at - lane_cell), 0.0)

    near = jnp.abs(b_at - l_at) <= RIM

    def circulant(row):
        full = pltpu.roll(jnp.broadcast_to(row, (128, 128)), 0, 1, stride=1, stride_axis=0)
        return jnp.where(near, full, 0.0).astype(BF16), jnp.where(near, 0.0, full).astype(BF16)

    def one_pair(k, carry):
        pair, shift = k // 8, lax.rem(k, 8)
        at_row = pl.multiple_of(shift * 256, 256)
        for half in range(2):
            tap = pair * 16 + half * 8 + shift
            same, other = circulant(rf[pl.ds(tap, 1), :])
            wf[pair, pl.ds(at_row, 128), half * 128:half * 128 + 128] = same
            wf[pair, pl.ds(at_row + 128, 128), half * 128:half * 128 + 128] = other
            same, other = circulant(ra[pl.ds(tap, 1), :])
            group = pair * 2 + half
            wa[group, pl.ds(at_row, 128), 0:128] = same
            wa[group, pl.ds(at_row, 128), 128:256] = other
            wa[group, pl.ds(at_row + 128, 128), 0:128] = other
            wa[group, pl.ds(at_row + 128, 128), 128:256] = same
        return carry

    lax.fori_loop(0, 32, one_pair, 0)

    of_global1(0).wait_recv()
    start_global2(0, global1_result(0))

    k_at, a_at = iota((128, 64), 0), iota((128, 64), 1)
    u_at = k_at // 5
    low_a = COARSE * (k_at - 5 * u_at - 2) - u_at + RIM
    rows_w = jnp.where((a_at >= low_a) & (a_at < low_a + COARSE), 1.0, 0.0).astype(BF16)
    x_at = -2 * COARSE - jnp.where(l_at < 16, l_at, l_at - 128)
    cols_w = jnp.where((b_at >= x_at + RIM) & (b_at < x_at + RIM + COARSE), 1.0, 0.0)
    fr[...] = dot(dot(rows_w, taps_h), cols_w, HI)
    j8 = iota((8, 128), 0)
    c8 = iota((8, 128), 1)
    xx = COARSE * (j8 - 2) - c8
    inside = (xx >= RIM - 84) & (xx <= RIM) & (c8 < TY)
    for u in range(COARSE):
        pieces = []
        for d in range(5):
            row = jnp.broadcast_to(fr[5 * u + d:5 * u + d + 1, :], (8, 128))
            row = pltpu.roll(pltpu.roll(row, 0, 1, stride=12, stride_axis=0), 0, 1, stride=13, stride_axis=0)
            pieces.append(jnp.where(inside, row, 0.0))
        pieces.append(jnp.zeros((8, 128), F32))
        block = jnp.concatenate(pieces, axis=0)
        for split in range(3):
            rounded = block.astype(BF16)
            vv[48 * split:48 * split + 48, 128 * u:128 * u + 128] = rounded
            block = block - rounded.astype(F32)

    et0[AIN + 8:, :] = jnp.zeros((EROWS - AIN - 8, 128), F32)
    et1[AIN + 8:, :] = jnp.zeros((EROWS - AIN - 8, 128), F32)
    ct0[AOUT:, :] = jnp.zeros((CROWS - AOUT, 128), F32)
    ct1[AOUT:, :] = jnp.zeros((CROWS - AOUT, 128), F32)

    of_halo(0).wait_recv()
    assemble(0, own[...])
    ct0[0:AOUT, :] = et0[32:32 + AOUT, :]
    ct1[0:AOUT, :] = et1[32:32 + AOUT, :]

    of_global2(0).wait_recv()
    set_back(global2_result(0))
    of_global1(0).wait_send()
    of_global2(0).wait_send()
    of_halo(0).wait_send()

    yes = lambda c: jnp.where(c, 1.0, 0.0).astype(F32)
    row_ok = jnp.ones((AOUT, 1), F32)
    r_at = iota((AOUT, 1), 0) - 32
    row_ok = jnp.where(r_at < 0, yes(s > 0), jnp.where(r_at >= TX, yes(s < ns - 1), 1.0))
    mask0 = jnp.where(lane < TY, 1.0, yes(n < nn - 1))
    mask1 = jnp.where(lane < 32, yes(n < nn - 1), yes(n > 0))

    def iteration(t, carry):
        for k in range(8):
            xb[:, 256 * k:256 * k + 128] = ct0[k + 2:k + 2 + BIN, :].astype(BF16)
            xb[:, 256 * k + 128:256 * k + 256] = ct1[k + 2:k + 2 + BIN, :].astype(BF16)
        blurred = None
        for pair in range(4):
            piece = dot(xb[...], wf[pair])
            lo = 16 * pair
            both = piece[lo:lo + TX, 0:128] + piece[lo + 8:lo + 8 + TX, 128:256]
            blurred = both if blurred is None else blurred + both
        exposure = blurred + bk[...]
        resist = jax.nn.sigmoid(GAIN * (exposure - LEVEL))
        own[:, 0:TY] = target_ref[...].astype(F32)
        error = (resist - own[...]) * GAIN * resist * (1.0 - resist)
        error = jnp.where(lane < TY, error, 0.0)
        err[...] = error
        half = error.astype(BF16).astype(F32)
        own[...] = half
        field_out(half)
        resist_ref[...] = resist[:, 0:TY]

        cells_in = jnp.concatenate(
            [own[pl.ds(u, CROW, stride=COARSE), :].astype(BF16) for u in range(COARSE)], axis=1)
        three = dot_nt(vv[...], cells_in)
        spread = three[0:40] + three[48:88] + three[96:136]
        cur_cols = jnp.where(lane < TY, col_sum(ct0.at[pl.ds(32, TX)]), 0.0)
        start_global1(t, payload(col_sum(err), cur_cols, spread))
        start_halo(t)

        of_global1(t).wait_recv()
        start_global2(t, global1_result(t))

        of_halo(t).wait_recv()
        assemble(t, own[...])
        for k in range(8):
            xa[:, 256 * k:256 * k + 128] = et0[k + 2:k + 2 + AIN, :].astype(BF16)
            xa[:, 256 * k + 128:256 * k + 256] = et1[k + 2:k + 2 + AIN, :].astype(BF16)
        for group in range(8):
            piece = dot(xa[...], wa[group])
            lo = 8 * group
            if group == 0:
                at0[...] = piece[lo:lo + AOUT, 0:128]
                at1[...] = piece[lo:lo + AOUT, 128:256]
            else:
                at0[...] += piece[lo:lo + AOUT, 0:128]
                at1[...] += piece[lo:lo + AOUT, 128:256]

        of_global2(t).wait_recv()
        out = global2_result(t)
        for u in range(COARSE):
            for ref, first in ((ub0, 0), (ub1, 128)):
                ref[pl.ds(6 + u, 8, stride=COARSE), :] = out[0:8, first:first + 128]
                ref[pl.ds(206 + u, 8, stride=COARSE), :] = out[8:16, first:first + 128]
        set_back(out)
        new0 = ct0[0:AOUT, :] - STEP * (at0[...] + ADJ_SCALE * ub0[24:24 + AOUT, :])
        new1 = ct1[0:AOUT, :] - STEP * (at1[...] + ADJ_SCALE * ub1[24:24 + AOUT, :])
        updated_ref[...] = new0[32:32 + TX, 0:TY]
        ct0[0:AOUT, :] = new0.astype(BF16).astype(F32) * (row_ok * mask0)
        ct1[0:AOUT, :] = new1.astype(BF16).astype(F32) * (row_ok * mask1)
        of_global1(t).wait_send()
        of_global2(t).wait_send()
        of_halo(t).wait_send()
        return carry

    lax.fori_loop(1, PHASES, iteration, 0)


def solution(mesh):
    ns, nn = mesh.shape["stripe"], mesh.shape["scan"]

    def per_device(dose, target, psf):
        vmem = pl.BlockSpec(memory_space=pltpu.VMEM)
        f = lambda *shape: pltpu.VMEM(shape, F32)
        h = lambda *shape: pltpu.VMEM(shape, BF16)
        return pl.pallas_call(
            lambda *refs: kernel(ns, nn, *refs),
            out_shape=(
                jax.ShapeDtypeStruct((TX, TY), F32),
                jax.ShapeDtypeStruct((TX, TY), F32),
            ),
            in_specs=[vmem] * 3,
            out_specs=(vmem, vmem),
            scratch_shapes=[
                f(PHASES, ns, 8, 128), f(PHASES, nn, 8, 128), h(PHASES, HALO, 128),
                h(SIDE, 128), h(EDGE, 128),
                f(EROWS, 128), f(EROWS, 128), f(CROWS, 128), f(CROWS, 128),
                f(AOUT, 128), f(AOUT, 128),
                h(8, 2048, 256), h(4, 2048, 256), h(144, 3200),
                f(64, 128), f(64, 128), f(64, 128), f(128, 128),
                h(AIN, 2048), h(BIN, 2048),
                f(TX, 128), f(TX, 128), f(40, 128), f(16, 128),
                f(128, 128), f(nn * 8, 512), f(416, 128), f(416, 128), f(TX, 128),
                pltpu.SemaphoreType.DMA((3,)), pltpu.SemaphoreType.DMA((PHASES, 3)),
            ],
            compiler_params=pltpu.CompilerParams(
                collective_id=0, has_side_effects=True, vmem_limit_bytes=60 << 20
            ),
            name="dose",
        )(dose, target, psf)

    return jax.shard_map(
        per_device, mesh=mesh,
        in_specs=(P("stripe", "scan"), P("stripe", "scan"), P()),
        out_specs=(P("stripe", "scan"), P("stripe", "scan")),
        check_vma=False,
    )
```

```python
import math

import jax
import jax.numpy as jnp
from jax import lax
from jax.experimental import pallas as pl
from jax.experimental.pallas import tpu as pltpu
from jax.sharding import PartitionSpec as P

TX, TY = 200, 100
TAPS = 61
COARSE = 25
SIGMA = 40
ITERS = 4
RIM = 30
BACK = 0.6
GAIN = 3.0
LEVEL = 1.5
STEP = 0.5
CROW, CCOL = TX // COARSE, TY // COARSE
ADJ_SCALE = BACK / (COARSE * COARSE)

MESH = pl.DeviceIdType.MESH
F32, BF16 = jnp.float32, jnp.bfloat16
HI = lax.Precision.HIGHEST

EROWS = 336
CROWS = 272
AOUT = 264
AIN = 320
BIN = 256
PHASES = ITERS + 1
SIDE = 208
EDGE = 64
HALO = 2 * SIDE + 6 * EDGE


def iota(shape, dim):
    return lax.broadcasted_iota(jnp.int32, shape, dim)


def dot(a, b, precision=None):
    return jnp.dot(a, b, precision=precision, preferred_element_type=F32)


def dot_nt(a, b, precision=None):
    return lax.dot_general(
        a, b, (((1,), (1,)), ((), ())), precision=precision, preferred_element_type=F32
    )


def gauss(dist):
    d = dist.astype(F32)
    return jnp.exp(-d * d / (2.0 * SIGMA * SIGMA)) / (math.sqrt(2.0 * math.pi) * SIGMA)


def cell_of(col):
    out = jnp.full(col.shape, -3, jnp.int32)
    for k in range(-2, 7):
        out = out + jnp.where(col >= COARSE * k, 1, 0)
    return out


def kernel(
    ns, nn, dose_ref, target_ref, psf_ref, resist_ref, updated_ref,
    g1, g2, halo, tile, bottom, et0, et1, ct0, ct1, at0, at1, wa, wf, vv,
    ps, rf, ra, fr, xa, xb, err, own, zs, sc, mw, cu, ub0, ub1, bk, bl,
    send_sem, recv_sem,
):
    s = lax.axis_index("stripe")
    n = lax.axis_index("scan")
    ncx, ncy = ns * CROW, nn * CCOL
    up, down = lax.rem(s + ns - 1, ns), lax.rem(s + 1, ns)
    left, right = lax.rem(n + nn - 1, nn), lax.rem(n + 1, nn)

    far = lambda count: sorted(range(1, count), key=lambda k: -min(k, count - k))
    barrier = pltpu.get_barrier_semaphore()

    def hello(a, b):
        pl.semaphore_signal(barrier, inc=1, device_id=(a, b), device_id_type=MESH)

    for a in (up, down):
        for b in (left, right):
            hello(a, b)
    for k in far(nn):
        hello(s, lax.rem(n + k, nn))
    for k in far(ns):
        hello(lax.rem(s + k, ns), n)

    lane = iota((1, 128), 1)

    def field_out(value):
        tile[0:TX, :] = value.astype(BF16)
        bottom[...] = value[TX - EDGE:, :].astype(BF16)

    def col_sum(ref):
        total = ref[pl.ds(0, CROW, stride=COARSE), :]
        for u in range(1, COARSE):
            total = total + ref[pl.ds(u, CROW, stride=COARSE), :]
        return total

    pick_row = iota((8, 128), 0)
    pick_cell = cell_of(iota((8, 128), 1))
    pick_in = iota((8, 128), 1) < TY
    pick_sum = jnp.where((pick_cell == pick_row) & pick_in, 1.0, 0.0)
    pick_dose = jnp.where((pick_cell == pick_row - 2) & pick_in, 1.0, 0.0)
    zs[...] = jnp.zeros_like(zs)
    sc[...] = jnp.zeros_like(sc)

    def sums_out(err_cols):
        sc[0:8, 0:8] = dot_nt(pick_sum, err_cols, HI)
        return pltpu.roll(jnp.where(lane < CROW, sc[0:8, :], 0.0), s * CROW, 1)

    def cells_out(cur_cols, spread):
        sc[8:16, 0:8] = dot_nt(pick_dose, cur_cols, HI)
        cells = pltpu.roll(jnp.where(lane < CROW, sc[8:16, :], 0.0), 64 + s * CROW, 1)
        cells = cells * (1.0 / (COARSE * COARSE))
        if spread is not None:
            zs[:, 0:8] = spread
            part = jnp.zeros((8, 128), F32)
            for d in range(5):
                part = part + pltpu.roll(zs[8 * d:8 * d + 8, :], 62 + d + s * CROW, 1)
            cells = cells - (STEP / (COARSE * COARSE)) * part
        return jnp.where(lane < 64, 0.0, cells)

    def start_stage1(which, t, value):
        g1[which, t, s] = value
        for k in far(ns):
            pltpu.make_async_remote_copy(
                g1.at[which, t, s], g1.at[which, t, s], send_sem.at[which], recv_sem.at[t, which],
                device_id=(lax.rem(s + k, ns), n), device_id_type=MESH,
            ).start()

    def start_stage2(which, t, value):
        g2[which, t, n] = value
        for k in far(nn):
            pltpu.make_async_remote_copy(
                g2.at[which, t, n], g2.at[which, t, n], send_sem.at[2 + which], recv_sem.at[t, 2 + which],
                device_id=(s, lax.rem(n + k, nn)), device_id_type=MESH,
            ).start()

    def start_halo(t):
        def go(src, first, rows, a, b):
            pltpu.make_async_remote_copy(
                src, halo.at[t, pl.ds(first, rows)], send_sem.at[4], recv_sem.at[t, 4],
                device_id=(a, b), device_id_type=MESH,
            ).start()

        top = tile.at[pl.ds(0, EDGE)]
        first = 2 * SIDE
        go(bottom, first + 2 * EDGE, EDGE, down, right)
        go(bottom, first + 3 * EDGE, EDGE, down, left)
        go(top, first + 4 * EDGE, EDGE, up, right)
        go(top, first + 5 * EDGE, EDGE, up, left)
        go(bottom, first, EDGE, down, n)
        go(top, first + EDGE, EDGE, up, n)
        go(tile, 0, SIDE, s, right)
        go(tile, SIDE, SIDE, s, left)

    def all_of(ref, sem_send, sem_recv):
        return pltpu.make_async_remote_copy(
            ref, ref, sem_send, sem_recv, device_id=(s, right), device_id_type=MESH
        )

    def of_stage1(which, t):
        return all_of(g1.at[which, t, pl.ds(0, ns - 1)], send_sem.at[which], recv_sem.at[t, which])

    def of_stage2(which, t):
        return all_of(g2.at[which, t, pl.ds(0, nn - 1)], send_sem.at[2 + which], recv_sem.at[t, 2 + which])

    def of_halo(t):
        return all_of(halo.at[t], send_sem.at[4], recv_sem.at[t, 4])

    def assemble(t, centre):
        yes = lambda c: jnp.where(c, 1.0, 0.0).astype(F32)
        has_up, has_down = yes(s > 0), yes(s < ns - 1)
        has_left, has_right = yes(n > 0), yes(n < nn - 1)
        first = 2 * SIDE

        def band(row, rows, mid, lhs, rhs, flag):
            lhs = pltpu.roll(lhs, 28, 1) * (has_left * flag)
            rhs = pltpu.roll(rhs, TY, 1) * (has_right * flag)
            et0[row:row + rows, :] = jnp.where(lane < TY, mid * flag, rhs)
            et1[row:row + rows, :] = jnp.where(lane < 32, rhs, jnp.where(lane >= 68, lhs, 0.0))

        def part(k, rows):
            return halo[t, pl.ds(k, rows), :].astype(F32)

        band(0, EDGE, part(first, EDGE), part(first + 2 * EDGE, EDGE), part(first + 3 * EDGE, EDGE), has_up)
        band(EDGE, TX, centre, part(0, TX), part(SIDE, TX), jnp.float32(1.0))
        band(EDGE + TX, EDGE, part(first + EDGE, EDGE), part(first + 4 * EDGE, EDGE), part(first + 5 * EDGE, EDGE), has_down)

    def rows_result(which, t):
        total = g1[which, t, 0]
        for k in range(1, ns):
            total = total + g1[which, t, k]
        parts = []
        for _ in range(3):
            parts.append(total.astype(BF16).astype(F32))
            total = total - parts[-1]
        parts.append(jnp.zeros_like(total))
        p = dot(jnp.concatenate(parts, axis=0).astype(BF16), mw[...])
        out = p[16:24, 0:128] + p[8:16, 128:256] + p[0:8, 256:384]
        out = out + p[8:16, 0:128] + p[0:8, 128:256]
        out = out + p[0:8, 0:128]
        row = iota((8, 128), 0)
        out = jnp.where(jnp.bitwise_and(row, 3) == iota((8, 128), 1) // 32, out, 0.0)
        return jnp.concatenate(
            [jnp.sum(out[0:4], axis=0, keepdims=True), jnp.sum(out[4:8], axis=0, keepdims=True)], axis=0)

    def turned_back(which, t):
        stack = jnp.concatenate([g2[which, t].reshape(nn * 2, 128), jnp.zeros((64, 128), F32)], axis=0)
        turned = jnp.transpose(stack)
        return jnp.concatenate(
            [turned[0:32] + pltpu.roll(turned[32:64], 64, 1), turned[64:96] + pltpu.roll(turned[96:128], 64, 1)],
            axis=1)

    def set_back(t, from_sums):
        value = dot(turned_back(1, t)[24:32], cu[:, 384:512], HI)
        value = BACK * (value if from_sums is None else value + from_sums)
        for u in range(COARSE):
            bk[pl.ds(u, CROW, stride=COARSE), :] = value

    def blur():
        for k in range(8):
            xb[:, 256 * k:256 * k + 128] = ct0[k + 2:k + 2 + BIN, :].astype(BF16)
            xb[:, 256 * k + 128:256 * k + 256] = ct1[k + 2:k + 2 + BIN, :].astype(BF16)
        blurred = None
        for pair in range(4):
            piece = dot(xb[...], wf[pair])
            lo = 16 * pair
            both = piece[lo:lo + TX, 0:128] + piece[lo + 8:lo + 8 + TX, 128:256]
            blurred = both if blurred is None else blurred + both
        bl[...] = blurred

    ps[...] = jnp.zeros_like(ps)
    ps[0:TAPS, 0:TAPS] = psf_ref[...].astype(F32)
    taps = ps[...]
    taps_h = taps.astype(BF16)
    b_at, l_at = iota((128, 128), 0), iota((128, 128), 1)
    perm_f = jnp.where((l_at == lax.rem(RIM - b_at + 256, 128)) & (b_at < TAPS), 1.0, 0.0).astype(BF16)
    perm_a = jnp.where((l_at == lax.rem(b_at - RIM + 256, 128)) & (b_at < TAPS), 1.0, 0.0).astype(BF16)
    flip = jnp.where(iota((64, 64), 1) == TAPS - 1 - iota((64, 64), 0), 1.0, 0.0).astype(BF16)
    rf[...] = dot(taps_h, perm_f)
    ra[...] = dot(dot(flip, taps_h).astype(BF16), perm_a)

    dose = jnp.zeros((TX, 128), F32)
    own[...] = dose
    own[:, 0:TY] = dose_ref[...].astype(F32)
    tile[...] = jnp.zeros_like(tile)
    field_out(own[...])
    first_payload = cells_out(col_sum(own), None)

    g_row = jnp.bitwise_and(b_at, 63)
    l32 = jnp.bitwise_and(l_at, 31)
    full_rows = gauss(iota((ncx, ncx), 0) - iota((ncx, ncx), 1))
    l64 = jnp.bitwise_and(iota((ncx, 128), 1), 31)
    twice = dot(full_rows, gauss(iota((ncx, 128), 0) - (s * CROW + l64 - 16)), HI)
    upper = jnp.concatenate([twice, jnp.zeros((128 - ncx, 128), F32)], axis=0)
    low = b_at < 64
    table = jnp.where(low & (l32 < 12), gauss(g_row - (s * CROW + l32 - 2)), 0.0)
    table = table + jnp.where(low & (l32 >= 16) & (l32 < 24), upper, 0.0)
    table = table + jnp.where((~low) & (l32 >= 24), gauss(g_row - (s * CROW + l32 - 24)), 0.0)
    table = jnp.where(g_row < ncx, table, 0.0)
    for k in range(3):
        rounded = table.astype(BF16)
        mw[:, 128 * k:128 * k + 128] = rounded
        table = table - rounded.astype(F32)
    mw[:, 384:512] = jnp.zeros((128, 128), BF16)

    k_at, a_at = iota((128, 64), 0), iota((128, 64), 1)
    u_at = k_at // 5
    low_a = COARSE * (k_at - 5 * u_at - 2) - u_at + RIM
    rows_w = jnp.where((a_at >= low_a) & (a_at < low_a + COARSE), 1.0, 0.0).astype(BF16)
    x_at = -2 * COARSE - jnp.where(l_at < 16, l_at, l_at - 128)
    cols_w = jnp.where((b_at >= x_at + RIM) & (b_at < x_at + RIM + COARSE), 1.0, 0.0)
    fr[...] = dot(dot(rows_w, taps_h), cols_w, HI)
    j8 = iota((8, 128), 0)
    c8 = iota((8, 128), 1)
    xx = COARSE * (j8 - 2) - c8
    inside = (xx >= RIM - 84) & (xx <= RIM) & (c8 < TY)
    for u in range(COARSE):
        pieces = []
        for d in range(5):
            row = jnp.broadcast_to(fr[5 * u + d:5 * u + d + 1, :], (8, 128))
            row = pltpu.roll(pltpu.roll(row, 0, 1, stride=12, stride_axis=0), 0, 1, stride=13, stride_axis=0)
            pieces.append(jnp.where(inside, row, 0.0))
        for d in range(5):
            top = pieces[d].astype(BF16).astype(F32)
            both = jnp.concatenate([top, pieces[d] - top], axis=0).astype(BF16)
            vv[16 * d:16 * d + 16, 128 * u:128 * u + 128] = both

    pl.semaphore_wait(barrier, ns - 1 + nn - 1 + 4)
    start_stage1(1, 0, first_payload)
    start_halo(0)

    near = jnp.abs(b_at - l_at) <= RIM

    def circulant(row):
        full = pltpu.roll(jnp.broadcast_to(row, (128, 128)), 0, 1, stride=1, stride_axis=0)
        return jnp.where(near, full, 0.0).astype(BF16), jnp.where(near, 0.0, full).astype(BF16)

    def one_pair(k, carry):
        pair, shift = k // 8, lax.rem(k, 8)
        at_row = pl.multiple_of(shift * 256, 256)
        for half in range(2):
            tap = pair * 16 + half * 8 + shift
            same, other = circulant(rf[pl.ds(tap, 1), :])
            wf[pair, pl.ds(at_row, 128), half * 128:half * 128 + 128] = same
            wf[pair, pl.ds(at_row + 128, 128), half * 128:half * 128 + 128] = other
            same, other = circulant(ra[pl.ds(tap, 1), :])
            group = pair * 2 + half
            wa[group, pl.ds(at_row, 128), 0:128] = same
            wa[group, pl.ds(at_row, 128), 128:256] = other
            wa[group, pl.ds(at_row + 128, 128), 0:128] = other
            wa[group, pl.ds(at_row + 128, 128), 128:256] = same
        return carry

    lax.fori_loop(0, 32, one_pair, 0)

    of_stage1(1, 0).wait_recv()
    start_stage2(1, 0, rows_result(1, 0))

    rows8 = nn * 8

    def q_dev(shape):
        at = iota(shape, 0)
        return 4 * jnp.bitwise_and(at, 1) + at // 64, jnp.bitwise_and(at, 63) // 2

    q, dev = q_dev((rows8, 256))
    pos = iota((rows8, 256), 1)
    col = jnp.where(pos < 160, pos, pos - 256)
    cu[:, 0:256] = jnp.where(q < CCOL, gauss(CCOL * dev + q - (CCOL * n + cell_of(col))), 0.0)
    q1, dev1 = q[:, 0:128], dev[:, 0:128]
    lane_cell = CCOL * n + cell_of(iota((rows8, 128), 1))
    mid_at = iota((ncy, 128), 0)
    mid = gauss(mid_at - (CCOL * n + cell_of(iota((ncy, 128), 1))))
    qf, devf = q_dev((rows8, ncy))
    outer = jnp.where(qf < CCOL, gauss(CCOL * (devf) + qf - iota((rows8, ncy), 1)), 0.0)
    cu[:, 256:384] = (-STEP * ADJ_SCALE) * dot(outer, mid, HI)
    at = CCOL * dev1 + q1 - 2
    cu[:, 384:512] = jnp.where((at >= 0) & (at < ncy), gauss(at - lane_cell), 0.0)


    et0[AIN + 8:, :] = jnp.zeros((EROWS - AIN - 8, 128), F32)
    et1[AIN + 8:, :] = jnp.zeros((EROWS - AIN - 8, 128), F32)
    ct0[AOUT:, :] = jnp.zeros((CROWS - AOUT, 128), F32)
    ct1[AOUT:, :] = jnp.zeros((CROWS - AOUT, 128), F32)

    of_halo(0).wait_recv()
    assemble(0, own[...])
    ct0[0:AOUT, :] = et0[32:32 + AOUT, :]
    ct1[0:AOUT, :] = et1[32:32 + AOUT, :]

    blur()
    of_stage2(1, 0).wait_recv()
    set_back(0, None)
    of_stage1(1, 0).wait_send()
    of_stage2(1, 0).wait_send()
    of_halo(0).wait_send()

    yes = lambda c: jnp.where(c, 1.0, 0.0).astype(F32)
    row_ok = jnp.ones((AOUT, 1), F32)
    r_at = iota((AOUT, 1), 0) - 32
    row_ok = jnp.where(r_at < 0, yes(s > 0), jnp.where(r_at >= TX, yes(s < ns - 1), 1.0))
    mask0 = jnp.where(lane < TY, 1.0, yes(n < nn - 1))
    mask1 = jnp.where(lane < 32, yes(n < nn - 1), yes(n > 0))

    def iteration(t, carry):
        exposure = bl[...] + bk[...]
        resist = jax.nn.sigmoid(GAIN * (exposure - LEVEL))
        own[:, 0:TY] = target_ref[...].astype(F32)
        error = (resist - own[...]) * GAIN * resist * (1.0 - resist)
        error = jnp.where(lane < TY, error, 0.0)
        err[...] = error
        half = error.astype(BF16).astype(F32)
        own[...] = half
        field_out(half)
        resist_ref[...] = resist[:, 0:TY]

        start_stage1(0, t, sums_out(col_sum(err)))
        start_halo(t)

        @pl.when(t < ITERS)
        def _():
            cells_in = jnp.concatenate(
                [own[pl.ds(u, CROW, stride=COARSE), :].astype(BF16) for u in range(COARSE)], axis=1)
            two = dot_nt(vv[...], cells_in)
            spread = jnp.concatenate([two[16 * d:16 * d + 8] + two[16 * d + 8:16 * d + 16] for d in range(5)], axis=0)
            cur_cols = jnp.where(lane < TY, col_sum(ct0.at[pl.ds(32, TX)]), 0.0)
            start_stage1(1, t, cells_out(cur_cols, spread))

        of_stage1(0, t).wait_recv()
        start_stage2(0, t, rows_result(0, t))

        @pl.when(t < ITERS)
        def _():
            of_stage1(1, t).wait_recv()
            start_stage2(1, t, rows_result(1, t))

        of_halo(t).wait_recv()
        assemble(t, own[...])
        for k in range(8):
            xa[:, 256 * k:256 * k + 128] = et0[k + 2:k + 2 + AIN, :].astype(BF16)
            xa[:, 256 * k + 128:256 * k + 256] = et1[k + 2:k + 2 + AIN, :].astype(BF16)
        for group in range(8):
            piece = dot(xa[...], wa[group])
            lo = 8 * group
            if group == 0:
                at0[...] = piece[lo:lo + AOUT, 0:128]
                at1[...] = piece[lo:lo + AOUT, 128:256]
            else:
                at0[...] += piece[lo:lo + AOUT, 0:128]
                at1[...] += piece[lo:lo + AOUT, 128:256]

        of_stage2(0, t).wait_recv()
        out = dot(turned_back(0, t), cu[:, 0:384], HI)
        for u in range(COARSE):
            for ref, first in ((ub0, 0), (ub1, 128)):
                ref[pl.ds(6 + u, 8, stride=COARSE), :] = out[0:8, first:first + 128]
                ref[pl.ds(206 + u, 8, stride=COARSE), :] = out[8:16, first:first + 128]
        new0 = ct0[0:AOUT, :] - STEP * (at0[...] + ADJ_SCALE * ub0[24:24 + AOUT, :])
        new1 = ct1[0:AOUT, :] - STEP * (at1[...] + ADJ_SCALE * ub1[24:24 + AOUT, :])
        updated_ref[...] = new0[32:32 + TX, 0:TY]
        ct0[0:AOUT, :] = new0.astype(BF16).astype(F32) * (row_ok * mask0)
        ct1[0:AOUT, :] = new1.astype(BF16).astype(F32) * (row_ok * mask1)

        @pl.when(t < ITERS)
        def _():
            blur()
            of_stage2(1, t).wait_recv()
            set_back(t, out[16:24, 256:384])
            of_stage1(1, t).wait_send()
            of_stage2(1, t).wait_send()

        of_stage1(0, t).wait_send()
        of_stage2(0, t).wait_send()
        of_halo(t).wait_send()
        return carry

    lax.fori_loop(1, PHASES, iteration, 0)


def solution(mesh):
    ns, nn = mesh.shape["stripe"], mesh.shape["scan"]

    def per_device(dose, target, psf):
        vmem = pl.BlockSpec(memory_space=pltpu.VMEM)
        f = lambda *shape: pltpu.VMEM(shape, F32)
        h = lambda *shape: pltpu.VMEM(shape, BF16)
        return pl.pallas_call(
            lambda *refs: kernel(ns, nn, *refs),
            out_shape=(
                jax.ShapeDtypeStruct((TX, TY), F32),
                jax.ShapeDtypeStruct((TX, TY), F32),
            ),
            in_specs=[vmem] * 3,
            out_specs=(vmem, vmem),
            scratch_shapes=[
                f(2, PHASES, ns, 8, 128), f(2, PHASES, nn, 2, 128), h(PHASES, HALO, 128),
                h(SIDE, 128), h(EDGE, 128),
                f(EROWS, 128), f(EROWS, 128), f(CROWS, 128), f(CROWS, 128),
                f(AOUT, 128), f(AOUT, 128),
                h(8, 2048, 256), h(4, 2048, 256), h(80, 3200),
                f(64, 128), f(64, 128), f(64, 128), f(128, 128),
                h(AIN, 2048), h(BIN, 2048),
                f(TX, 128), f(TX, 128), f(40, 128), f(16, 128),
                h(128, 512), f(nn * 8, 512), f(416, 128), f(416, 128), f(TX, 128), f(TX, 128),
                pltpu.SemaphoreType.DMA((5,)), pltpu.SemaphoreType.DMA((PHASES, 5)),
            ],
            compiler_params=pltpu.CompilerParams(
                collective_id=0, has_side_effects=True, vmem_limit_bytes=60 << 20
            ),
            name="dose",
        )(dose, target, psf)

    return jax.shard_map(
        per_device, mesh=mesh,
        in_specs=(P("stripe", "scan"), P("stripe", "scan"), P()),
        out_specs=(P("stripe", "scan"), P("stripe", "scan")),
        check_vma=False,
    )
```

```python
import math

import jax
import jax.numpy as jnp
from jax import lax
from jax.experimental import pallas as pl
from jax.experimental.pallas import tpu as pltpu
from jax.sharding import PartitionSpec as P

TX, TY = 200, 100
TAPS = 61
COARSE = 25
SIGMA = 40
ITERS = 4
RIM = 30
BACK = 0.6
GAIN = 3.0
LEVEL = 1.5
STEP = 0.5
CROW, CCOL = TX // COARSE, TY // COARSE
ADJ_SCALE = BACK / (COARSE * COARSE)

MESH = pl.DeviceIdType.MESH
F32, BF16 = jnp.float32, jnp.bfloat16
HI = lax.Precision.HIGHEST

EROWS = 336
CROWS = 272
AOUT = 264
AIN = 320
BIN = 256
PHASES = ITERS + 1
SIDE = 112
SIDE_ROWS = 104
CORNER = 32
EDGE = 64
AT = (0, SIDE, 2 * SIDE, 2 * SIDE + CORNER, 2 * SIDE + 2 * CORNER, 2 * SIDE + 3 * CORNER,
      2 * SIDE + 4 * CORNER, 2 * SIDE + 4 * CORNER + EDGE)
HALO = 2 * SIDE + 4 * CORNER + 2 * EDGE


def iota(shape, dim):
    return lax.broadcasted_iota(jnp.int32, shape, dim)


def dot(a, b, precision=None):
    return jnp.dot(a, b, precision=precision, preferred_element_type=F32)


def dot_nt(a, b, precision=None):
    return lax.dot_general(
        a, b, (((1,), (1,)), ((), ())), precision=precision, preferred_element_type=F32
    )


def gauss(dist):
    d = dist.astype(F32)
    return jnp.exp(-d * d / (2.0 * SIGMA * SIGMA)) / (math.sqrt(2.0 * math.pi) * SIGMA)


def cell_of(col):
    out = jnp.full(col.shape, -3, jnp.int32)
    for k in range(-2, 7):
        out = out + jnp.where(col >= COARSE * k, 1, 0)
    return out


def kernel(
    ns, nn, dose_ref, target_ref, psf_ref, resist_ref, updated_ref,
    g1, g2, halo, tile, et0, et1, ct0, ct1, at0, at1, wa, wf, vv,
    ps, rf, ra, fr, xa, xb, err, own, zs, sc, mw, cu, cb, ub0, ub1, bk, bl,
    send_sem, recv_sem,
):
    s = lax.axis_index("stripe")
    n = lax.axis_index("scan")
    ncx, ncy = ns * CROW, nn * CCOL
    up, down = lax.rem(s + ns - 1, ns), lax.rem(s + 1, ns)
    left, right = lax.rem(n + nn - 1, nn), lax.rem(n + 1, nn)

    x_lo = lax.rem(n // 2, 2)
    core = lax.rem(n, 2)
    far = lambda count: sorted(range(count), key=lambda k: -min(k, count - k))
    plane, column = [], []
    for k in far(ns):
        for flip in (1, 0):
            if k or flip:
                plane.append((lax.rem(s + k, ns), n + 2 * flip * (1 - 2 * x_lo)))
    for k in far(nn // 4):
        for flip in (1, 0):
            if k or flip:
                column.append((s, lax.rem(n + 4 * k, nn) + flip * (1 - 2 * core)))
    own1, own2 = x_lo * ns + s, (n // 4) * 2 + core
    barrier = pltpu.get_barrier_semaphore()

    def hello(a, b):
        pl.semaphore_signal(barrier, inc=1, device_id=(a, b), device_id_type=MESH)

    for a in (up, down):
        for b in (left, right):
            hello(a, b)
    for b in (left, right):
        hello(s, b)
    for a, b in plane + column:
        hello(a, b)

    lane = iota((1, 128), 1)

    def fold(value):
        half = value.shape[0] // 2
        return jnp.where(lane < 64, value[0:half], pltpu.roll(value[half:], 64, 1)).astype(BF16)

    def field_out(value):
        last = pltpu.roll(value, 92, 1)
        more = jnp.zeros((2 * SIDE_ROWS - TX, 128), F32)
        tile[AT[0]:AT[0] + SIDE_ROWS, :] = fold(jnp.concatenate([last, more], axis=0))
        tile[AT[1]:AT[1] + SIDE_ROWS, :] = fold(jnp.concatenate([value, more], axis=0))
        tile[AT[2]:AT[2] + CORNER, :] = fold(last[TX - EDGE:])
        tile[AT[3]:AT[3] + CORNER, :] = fold(value[TX - EDGE:])
        tile[AT[4]:AT[4] + CORNER, :] = fold(last[0:EDGE])
        tile[AT[5]:AT[5] + CORNER, :] = fold(value[0:EDGE])
        tile[AT[6]:AT[6] + EDGE, :] = value[TX - EDGE:].astype(BF16)
        tile[AT[7]:AT[7] + EDGE, :] = value[0:EDGE].astype(BF16)

    def col_sum(ref):
        total = ref[pl.ds(0, CROW, stride=COARSE), :]
        for u in range(1, COARSE):
            total = total + ref[pl.ds(u, CROW, stride=COARSE), :]
        return total

    pick_row = iota((8, 128), 0)
    pick_cell = cell_of(iota((8, 128), 1))
    pick_in = iota((8, 128), 1) < TY
    pick_sum = jnp.where((pick_cell == pick_row) & pick_in, 1.0, 0.0)
    pick_dose = jnp.where((pick_cell == pick_row - 2) & pick_in, 1.0, 0.0)
    zs[...] = jnp.zeros_like(zs)
    sc[...] = jnp.zeros_like(sc)

    def sums_out(err_cols):
        parts = []
        for _ in range(3):
            parts.append(err_cols.astype(BF16).astype(F32))
            err_cols = err_cols - parts[-1]
        parts.append(jnp.zeros_like(err_cols))
        picks = jnp.concatenate([pick_sum, jnp.zeros_like(pick_sum)], axis=0).astype(BF16)
        sc[:, 0:32] = dot_nt(picks, jnp.concatenate(parts, axis=0).astype(BF16))
        got = sc[0:8, :]
        got = got + (pltpu.roll(got, 128 - CROW, 1) + pltpu.roll(got, 128 - 2 * CROW, 1))
        return pltpu.roll(jnp.where(lane < CROW, got, 0.0), s * CROW, 1)

    def cells_out(cur_cols, spread):
        sc[8:16, 0:8] = dot_nt(pick_dose, cur_cols, HI)
        cells = pltpu.roll(jnp.where(lane < CROW, sc[8:16, :], 0.0), 64 + s * CROW, 1)
        cells = cells * (1.0 / (COARSE * COARSE))
        if spread is not None:
            zs[:, 0:8] = spread
            part = jnp.zeros((8, 128), F32)
            for d in range(5):
                part = part + pltpu.roll(zs[8 * d:8 * d + 8, :], 62 + d + s * CROW, 1)
            cells = cells - (STEP / (COARSE * COARSE)) * part
        return jnp.where(lane < 64, 0.0, cells)

    def start_stage1(which, t, value):
        g1[which, t, own1] = value
        for a, b in plane:
            pltpu.make_async_remote_copy(
                g1.at[which, t, own1], g1.at[which, t, own1], send_sem.at[which], recv_sem.at[t, which],
                device_id=(a, b), device_id_type=MESH,
            ).start()

    def start_stage2(which, t, value):
        g2[which, t, own2] = value
        for a, b in column:
            pltpu.make_async_remote_copy(
                g2.at[which, t, own2], g2.at[which, t, own2], send_sem.at[2 + which], recv_sem.at[t, 2 + which],
                device_id=(a, b), device_id_type=MESH,
            ).start()

    def start_halo(t):
        sizes = (SIDE, SIDE, CORNER, CORNER, CORNER, CORNER, EDGE, EDGE)
        to = ((s, right), (s, left), (down, right), (down, left), (up, right), (up, left), (down, n), (up, n))
        for k in (2, 3, 4, 5, 6, 7, 0, 1):
            part = pl.ds(AT[k], sizes[k])
            pltpu.make_async_remote_copy(
                tile.at[part], halo.at[t, part], send_sem.at[4], recv_sem.at[t, 4],
                device_id=to[k], device_id_type=MESH,
            ).start()

    def all_of(ref, sem_send, sem_recv):
        return pltpu.make_async_remote_copy(
            ref, ref, sem_send, sem_recv, device_id=(s, right), device_id_type=MESH
        )

    def of_stage1(which, t):
        return all_of(g1.at[which, t, pl.ds(0, 2 * ns - 1)], send_sem.at[which], recv_sem.at[t, which])

    def of_stage2(which, t):
        return all_of(g2.at[which, t, pl.ds(0, nn // 2 - 1)], send_sem.at[2 + which], recv_sem.at[t, 2 + which])

    def of_halo(t):
        return all_of(halo.at[t], send_sem.at[4], recv_sem.at[t, 4])

    def assemble(t, centre):
        yes = lambda c: jnp.where(c, 1.0, 0.0).astype(F32)
        has_up, has_down = yes(s > 0), yes(s < ns - 1)
        has_left, has_right = yes(n > 0), yes(n < nn - 1)

        def band(row, rows, mid, lhs, rhs, flag):
            lhs = jnp.concatenate([pltpu.roll(lhs, 64, 1), lhs], axis=0)[0:rows] * (has_left * flag)
            rhs = jnp.concatenate([pltpu.roll(rhs, TY, 1), pltpu.roll(rhs, 36, 1)], axis=0)[0:rows] * (has_right * flag)
            et0[row:row + rows, :] = jnp.where(lane < TY, mid * flag, rhs)
            et1[row:row + rows, :] = jnp.where(lane < 32, rhs, jnp.where(lane >= 68, lhs, 0.0))

        def part(k, rows):
            return halo[t, pl.ds(AT[k], rows), :].astype(F32)

        band(0, EDGE, part(6, EDGE), part(2, CORNER), part(3, CORNER), has_up)
        band(EDGE, TX, centre, part(0, SIDE_ROWS), part(1, SIDE_ROWS), jnp.float32(1.0))
        band(EDGE + TX, EDGE, part(7, EDGE), part(4, CORNER), part(5, CORNER), has_down)

    def rows_result(which, t):
        totals = []
        for x in range(2):
            total = g1[which, t, x * ns]
            for k in range(1, ns):
                total = total + g1[which, t, x * ns + k]
            totals.append(total)
        total = jnp.concatenate(totals, axis=0)
        parts = []
        for _ in range(3):
            parts.append(total.astype(BF16).astype(F32))
            total = total - parts[-1]
        p = dot(jnp.concatenate(parts, axis=0).astype(BF16), mw[...])
        out = p[32:48, 0:128] + p[16:32, 128:256] + p[0:16, 256:384]
        out = out + p[16:32, 0:128] + p[0:16, 128:256]
        out = out + p[0:16, 0:128]
        row = iota((16, 128), 0)
        out = jnp.where(jnp.bitwise_and(row, 3) == iota((16, 128), 1) // 32, out, 0.0)
        return jnp.concatenate([jnp.sum(out[4 * k:4 * k + 4], axis=0, keepdims=True) for k in range(4)], axis=0)

    def turned_back(which, t):
        stack = jnp.concatenate([g2[which, t].reshape(nn * 2, 128), jnp.zeros((64, 128), F32)], axis=0)
        turned = jnp.transpose(stack)
        return jnp.concatenate(
            [turned[0:32] + pltpu.roll(turned[32:64], 64, 1), turned[64:96] + pltpu.roll(turned[96:128], 64, 1)],
            axis=1)

    def dot_cols(lhs, first, last):
        rows = lhs.shape[0]
        parts = []
        for _ in range(3):
            parts.append(lhs.astype(BF16).astype(F32))
            lhs = lhs - parts[-1]
        p = dot(jnp.concatenate(parts, axis=0).astype(BF16), cb[0, :, first:last])
        q2 = dot(jnp.concatenate(parts[0:2], axis=0).astype(BF16), cb[1, :, first:last])
        q3 = dot(parts[0].astype(BF16), cb[2, :, first:last])
        out = p[2 * rows:] + q2[rows:] + q3
        out = out + p[rows:2 * rows] + q2[0:rows]
        return out + p[0:rows]

    def set_back(t, from_sums):
        value = dot_cols(turned_back(1, t)[24:32], 384, 512)
        value = BACK * (value if from_sums is None else value + from_sums)
        for u in range(COARSE):
            bk[pl.ds(u, CROW, stride=COARSE), :] = value

    def blur():
        for k in range(8):
            xb[:, 256 * k:256 * k + 128] = ct0[k + 2:k + 2 + BIN, :].astype(BF16)
            xb[:, 256 * k + 128:256 * k + 256] = ct1[k + 2:k + 2 + BIN, :].astype(BF16)
        blurred = None
        for pair in range(4):
            piece = dot(xb[...], wf[pair])
            lo = 16 * pair
            both = piece[lo:lo + TX, 0:128] + piece[lo + 8:lo + 8 + TX, 128:256]
            blurred = both if blurred is None else blurred + both
        bl[...] = blurred

    ps[...] = jnp.zeros_like(ps)
    ps[0:TAPS, 0:TAPS] = psf_ref[...].astype(F32)
    taps = ps[...]
    taps_h = taps.astype(BF16)
    b_at, l_at = iota((128, 128), 0), iota((128, 128), 1)
    perm_f = jnp.where((l_at == lax.rem(RIM - b_at + 256, 128)) & (b_at < TAPS), 1.0, 0.0).astype(BF16)
    perm_a = jnp.where((l_at == lax.rem(b_at - RIM + 256, 128)) & (b_at < TAPS), 1.0, 0.0).astype(BF16)
    flip = jnp.where(iota((64, 64), 1) == TAPS - 1 - iota((64, 64), 0), 1.0, 0.0).astype(BF16)
    rf[...] = dot(taps_h, perm_f)
    ra[...] = dot(dot(flip, taps_h).astype(BF16), perm_a)

    dose = jnp.zeros((TX, 128), F32)
    own[...] = dose
    own[:, 0:TY] = dose_ref[...].astype(F32)
    tile[...] = jnp.zeros_like(tile)
    field_out(own[...])
    first_payload = cells_out(col_sum(own), None)

    g_row = jnp.bitwise_and(b_at, 63)
    l32 = jnp.bitwise_and(l_at, 31)
    full_rows = gauss(iota((ncx, ncx), 0) - iota((ncx, ncx), 1))
    l64 = jnp.bitwise_and(iota((ncx, 128), 1), 31)
    twice = dot(full_rows, gauss(iota((ncx, 128), 0) - (s * CROW + l64 - 16)), HI)
    upper = jnp.concatenate([twice, jnp.zeros((128 - ncx, 128), F32)], axis=0)
    low = b_at < 64
    table = jnp.where(low & (l32 < 12), gauss(g_row - (s * CROW + l32 - 2)), 0.0)
    table = table + jnp.where(low & (l32 >= 16) & (l32 < 24), upper, 0.0)
    table = table + jnp.where((~low) & (l32 >= 24), gauss(g_row - (s * CROW + l32 - 24)), 0.0)
    table = jnp.where(g_row < ncx, table, 0.0)
    for k in range(3):
        rounded = table.astype(BF16)
        mw[:, 128 * k:128 * k + 128] = rounded
        table = table - rounded.astype(F32)
    mw[:, 384:512] = jnp.zeros((128, 128), BF16)

    k_at, a_at = iota((128, 64), 0), iota((128, 64), 1)
    u_at = k_at // 5
    low_a = COARSE * (k_at - 5 * u_at - 2) - u_at + RIM
    rows_w = jnp.where((a_at >= low_a) & (a_at < low_a + COARSE), 1.0, 0.0).astype(BF16)
    x_at = -2 * COARSE - jnp.where(l_at < 16, l_at, l_at - 128)
    cols_w = jnp.where((b_at >= x_at + RIM) & (b_at < x_at + RIM + COARSE), 1.0, 0.0)
    fr[...] = dot(dot(rows_w, taps_h), cols_w, HI)
    j8 = iota((8, 128), 0)
    c8 = iota((8, 128), 1)
    xx = COARSE * (j8 - 2) - c8
    inside = (xx >= RIM - 84) & (xx <= RIM) & (c8 < TY)
    for u in range(COARSE):
        pieces = []
        for d in range(5):
            row = jnp.broadcast_to(fr[5 * u + d:5 * u + d + 1, :], (8, 128))
            row = pltpu.roll(pltpu.roll(row, 0, 1, stride=12, stride_axis=0), 0, 1, stride=13, stride_axis=0)
            pieces.append(jnp.where(inside, row, 0.0))
        for d in range(5):
            top = pieces[d].astype(BF16).astype(F32)
            both = jnp.concatenate([top, pieces[d] - top], axis=0).astype(BF16)
            vv[16 * d:16 * d + 16, 128 * u:128 * u + 128] = both

    pl.semaphore_wait(barrier, len(plane) + len(column) + 6)
    start_stage1(1, 0, first_payload)
    start_halo(0)

    near = jnp.abs(b_at - l_at) <= RIM

    def circulant(row):
        full = pltpu.roll(jnp.broadcast_to(row, (128, 128)), 0, 1, stride=1, stride_axis=0)
        return jnp.where(near, full, 0.0).astype(BF16), jnp.where(near, 0.0, full).astype(BF16)

    def one_pair(k, carry):
        pair, shift = k // 8, lax.rem(k, 8)
        at_row = pl.multiple_of(shift * 256, 256)
        for half in range(2):
            tap = pair * 16 + half * 8 + shift
            same, other = circulant(rf[pl.ds(tap, 1), :])
            wf[pair, pl.ds(at_row, 128), half * 128:half * 128 + 128] = same
            wf[pair, pl.ds(at_row + 128, 128), half * 128:half * 128 + 128] = other
            same, other = circulant(ra[pl.ds(tap, 1), :])
            group = pair * 2 + half
            wa[group, pl.ds(at_row, 128), 0:128] = same
            wa[group, pl.ds(at_row, 128), 128:256] = other
            wa[group, pl.ds(at_row + 128, 128), 0:128] = other
            wa[group, pl.ds(at_row + 128, 128), 128:256] = same
        return carry

    lax.fori_loop(0, 32, one_pair, 0)

    of_stage1(1, 0).wait_recv()
    start_stage2(1, 0, rows_result(1, 0))

    rows8 = nn * 8

    def q_dev(shape):
        at = iota(shape, 0)
        pos = jnp.bitwise_and(at, 63)
        z, c, x = pos // 8, jnp.bitwise_and(pos // 4, 1), jnp.bitwise_and(pos // 2, 1)
        return 4 * jnp.bitwise_and(at, 1) + at // 64, 4 * z + 2 * x + c

    q, dev = q_dev((rows8, 256))
    pos = iota((rows8, 256), 1)
    col = jnp.where(pos < 160, pos, pos - 256)
    cu[:, 0:256] = jnp.where(q < CCOL, gauss(CCOL * dev + q - (CCOL * n + cell_of(col))), 0.0)
    q1, dev1 = q[:, 0:128], dev[:, 0:128]
    lane_cell = CCOL * n + cell_of(iota((rows8, 128), 1))
    mid_at = iota((ncy, 128), 0)
    mid = gauss(mid_at - (CCOL * n + cell_of(iota((ncy, 128), 1))))
    qf, devf = q_dev((rows8, ncy))
    outer = jnp.where(qf < CCOL, gauss(CCOL * (devf) + qf - iota((rows8, ncy), 1)), 0.0)
    cu[:, 256:384] = (-STEP * ADJ_SCALE) * dot(outer, mid, HI)
    at = CCOL * dev1 + q1 - 2
    cu[:, 384:512] = jnp.where((at >= 0) & (at < ncy), gauss(at - lane_cell), 0.0)
    rest = cu[...]
    for k in range(3):
        cb[k] = rest.astype(BF16)
        rest = rest - cb[k].astype(F32)


    et0[AIN + 8:, :] = jnp.zeros((EROWS - AIN - 8, 128), F32)
    et1[AIN + 8:, :] = jnp.zeros((EROWS - AIN - 8, 128), F32)
    ct0[AOUT:, :] = jnp.zeros((CROWS - AOUT, 128), F32)
    ct1[AOUT:, :] = jnp.zeros((CROWS - AOUT, 128), F32)

    of_halo(0).wait_recv()
    assemble(0, own[...])
    ct0[0:AOUT, :] = et0[32:32 + AOUT, :]
    ct1[0:AOUT, :] = et1[32:32 + AOUT, :]

    blur()
    of_stage2(1, 0).wait_recv()
    set_back(0, None)
    of_stage1(1, 0).wait_send()
    of_stage2(1, 0).wait_send()
    of_halo(0).wait_send()

    yes = lambda c: jnp.where(c, 1.0, 0.0).astype(F32)
    row_ok = jnp.ones((AOUT, 1), F32)
    r_at = iota((AOUT, 1), 0) - 32
    row_ok = jnp.where(r_at < 0, yes(s > 0), jnp.where(r_at >= TX, yes(s < ns - 1), 1.0))
    mask0 = jnp.where(lane < TY, 1.0, yes(n < nn - 1))
    mask1 = jnp.where(lane < 32, yes(n < nn - 1), yes(n > 0))

    def iteration(t, carry):
        exposure = bl[...] + bk[...]
        resist = jax.nn.sigmoid(GAIN * (exposure - LEVEL))
        own[:, 0:TY] = target_ref[...].astype(F32)
        error = (resist - own[...]) * GAIN * resist * (1.0 - resist)
        error = jnp.where(lane < TY, error, 0.0)
        err[...] = error
        half = error.astype(BF16).astype(F32)
        own[...] = half
        field_out(half)
        resist_ref[...] = resist[:, 0:TY]

        start_stage1(0, t, sums_out(col_sum(err)))
        @pl.when(t < ITERS)
        def _():
            cells_in = jnp.concatenate(
                [own[pl.ds(u, CROW, stride=COARSE), :].astype(BF16) for u in range(COARSE)], axis=1)
            two = dot_nt(vv[...], cells_in)
            spread = jnp.concatenate([two[16 * d:16 * d + 8] + two[16 * d + 8:16 * d + 16] for d in range(5)], axis=0)
            cur_cols = jnp.where(lane < TY, col_sum(ct0.at[pl.ds(32, TX)]), 0.0)
            start_stage1(1, t, cells_out(cur_cols, spread))

        start_halo(t)

        of_stage1(0, t).wait_recv()
        start_stage2(0, t, rows_result(0, t))

        @pl.when(t < ITERS)
        def _():
            of_stage1(1, t).wait_recv()
            start_stage2(1, t, rows_result(1, t))

        of_halo(t).wait_recv()
        assemble(t, own[...])
        for k in range(8):
            xa[:, 256 * k:256 * k + 128] = et0[k + 2:k + 2 + AIN, :].astype(BF16)
            xa[:, 256 * k + 128:256 * k + 256] = et1[k + 2:k + 2 + AIN, :].astype(BF16)
        for group in range(8):
            piece = dot(xa[...], wa[group])
            lo = 8 * group
            if group == 0:
                at0[...] = piece[lo:lo + AOUT, 0:128]
                at1[...] = piece[lo:lo + AOUT, 128:256]
            else:
                at0[...] += piece[lo:lo + AOUT, 0:128]
                at1[...] += piece[lo:lo + AOUT, 128:256]

        of_stage2(0, t).wait_recv()
        turned = turned_back(0, t)
        out = dot_cols(turned[0:16], 0, 256)
        for u in range(COARSE):
            for ref, first in ((ub0, 0), (ub1, 128)):
                ref[pl.ds(6 + u, 8, stride=COARSE), :] = out[0:8, first:first + 128]
                ref[pl.ds(206 + u, 8, stride=COARSE), :] = out[8:16, first:first + 128]
        new0 = ct0[0:AOUT, :] - STEP * (at0[...] + ADJ_SCALE * ub0[24:24 + AOUT, :])
        new1 = ct1[0:AOUT, :] - STEP * (at1[...] + ADJ_SCALE * ub1[24:24 + AOUT, :])
        updated_ref[...] = new0[32:32 + TX, 0:TY]
        ct0[0:AOUT, :] = new0.astype(BF16).astype(F32) * (row_ok * mask0)
        ct1[0:AOUT, :] = new1.astype(BF16).astype(F32) * (row_ok * mask1)

        @pl.when(t < ITERS)
        def _():
            blur()
            from_sums = dot_cols(turned[16:24], 256, 384)
            of_stage2(1, t).wait_recv()
            set_back(t, from_sums)
            of_stage1(1, t).wait_send()
            of_stage2(1, t).wait_send()

        of_stage1(0, t).wait_send()
        of_stage2(0, t).wait_send()
        of_halo(t).wait_send()
        return carry

    lax.fori_loop(1, PHASES, iteration, 0)


def solution(mesh):
    ns, nn = mesh.shape["stripe"], mesh.shape["scan"]

    def per_device(dose, target, psf):
        vmem = pl.BlockSpec(memory_space=pltpu.VMEM)
        f = lambda *shape: pltpu.VMEM(shape, F32)
        h = lambda *shape: pltpu.VMEM(shape, BF16)
        return pl.pallas_call(
            lambda *refs: kernel(ns, nn, *refs),
            out_shape=(
                jax.ShapeDtypeStruct((TX, TY), F32),
                jax.ShapeDtypeStruct((TX, TY), F32),
            ),
            in_specs=[vmem] * 3,
            out_specs=(vmem, vmem),
            scratch_shapes=[
                f(2, PHASES, 2 * ns, 8, 128), f(2, PHASES, nn // 2, 4, 128), h(PHASES, HALO, 128),
                h(HALO, 128),
                f(EROWS, 128), f(EROWS, 128), f(CROWS, 128), f(CROWS, 128),
                f(AOUT, 128), f(AOUT, 128),
                h(8, 2048, 256), h(4, 2048, 256), h(80, 3200),
                f(64, 128), f(64, 128), f(64, 128), f(128, 128),
                h(AIN, 2048), h(BIN, 2048),
                f(TX, 128), f(TX, 128), f(40, 128), f(16, 128),
                h(128, 512), f(nn * 8, 512), h(3, nn * 8, 512), f(416, 128), f(416, 128), f(TX, 128), f(TX, 128),
                pltpu.SemaphoreType.DMA((5,)), pltpu.SemaphoreType.DMA((PHASES, 5)),
            ],
            compiler_params=pltpu.CompilerParams(
                collective_id=0, has_side_effects=True, vmem_limit_bytes=60 << 20
            ),
            name="dose",
        )(dose, target, psf)

    return jax.shard_map(
        per_device, mesh=mesh,
        in_specs=(P("stripe", "scan"), P("stripe", "scan"), P()),
        out_specs=(P("stripe", "scan"), P("stripe", "scan")),
        check_vma=False,
    )
```

```python
import math

import jax
import jax.numpy as jnp
from jax import lax
from jax.experimental import pallas as pl
from jax.experimental.pallas import tpu as pltpu
from jax.sharding import PartitionSpec as P

TX, TY = 200, 100
TAPS = 61
COARSE = 25
SIGMA = 40
ITERS = 4
RIM = 30
BACK = 0.6
GAIN = 3.0
LEVEL = 1.5
STEP = 0.5
CROW, CCOL = TX // COARSE, TY // COARSE
ADJ_SCALE = BACK / (COARSE * COARSE)

MESH = pl.DeviceIdType.MESH
F32, BF16 = jnp.float32, jnp.bfloat16
HI = lax.Precision.HIGHEST

EROWS = 336
CROWS = 272
AOUT = 264
AIN = 320
BIN = 256
PHASES = ITERS + 1
SIDE = 112
SIDE_ROWS = 104
CORNER = 32
EDGE = 64
AT = (0, SIDE, 2 * SIDE, 2 * SIDE + CORNER, 2 * SIDE + 2 * CORNER, 2 * SIDE + 3 * CORNER,
      2 * SIDE + 4 * CORNER, 2 * SIDE + 4 * CORNER + EDGE)
HALO = 2 * SIDE + 4 * CORNER + 2 * EDGE


def iota(shape, dim):
    return lax.broadcasted_iota(jnp.int32, shape, dim)


def dot(a, b, precision=None):
    return jnp.dot(a, b, precision=precision, preferred_element_type=F32)


def dot_nt(a, b, precision=None):
    return lax.dot_general(
        a, b, (((1,), (1,)), ((), ())), precision=precision, preferred_element_type=F32
    )


def gauss(dist):
    d = dist.astype(F32)
    return jnp.exp(-d * d / (2.0 * SIGMA * SIGMA)) / (math.sqrt(2.0 * math.pi) * SIGMA)


def cell_of(col):
    out = jnp.full(col.shape, -3, jnp.int32)
    for k in range(-2, 7):
        out = out + jnp.where(col >= COARSE * k, 1, 0)
    return out


def kernel(
    ns, nn, dose_ref, target_ref, psf_ref, both_ref,
    gs1, gd1, gs2, gd2, halo, tile, et0, et1, ct0, ct1, at0, at1, wa, wf, vv,
    ps, rf, ra, fr, xa, xb, err, own, zs, sc, mw, ts, td, ub0, ub1, bk, bl,
    send_sem, recv_sem,
):
    s = lax.axis_index("stripe")
    n = lax.axis_index("scan")
    ncx, ncy = ns * CROW, nn * CCOL
    up, down = lax.rem(s + ns - 1, ns), lax.rem(s + 1, ns)
    left, right = lax.rem(n + nn - 1, nn), lax.rem(n + 1, nn)

    x_lo = lax.rem(n // 2, 2)
    core = lax.rem(n, 2)
    far = lambda count: sorted(range(count), key=lambda k: -min(k, count - k))
    plane, column = [], []
    for k in far(ns):
        for flip in (1, 0):
            if k or flip:
                plane.append((lax.rem(s + k, ns), n + 2 * flip * (1 - 2 * x_lo)))
    for k in far(nn // 4):
        for flip in (1, 0):
            if k or flip:
                column.append((s, lax.rem(n + 4 * k, nn) + flip * (1 - 2 * core)))
    own1, own2 = x_lo * ns + s, (n // 4) * 2 + core
    barrier = pltpu.get_barrier_semaphore()

    def hello(a, b):
        pl.semaphore_signal(barrier, inc=1, device_id=(a, b), device_id_type=MESH)

    for a in (up, down):
        for b in (left, right):
            hello(a, b)
    for b in (left, right):
        hello(s, b)
    for a, b in plane + column:
        hello(a, b)

    lane = iota((1, 128), 1)

    def fold(value):
        half = value.shape[0] // 2
        return jnp.where(lane < 64, value[0:half], pltpu.roll(value[half:], 64, 1)).astype(BF16)

    def field_out(value):
        last = pltpu.roll(value, 92, 1)
        more = jnp.zeros((2 * SIDE_ROWS - TX, 128), F32)
        tile[AT[0]:AT[0] + SIDE_ROWS, :] = fold(jnp.concatenate([last, more], axis=0))
        tile[AT[1]:AT[1] + SIDE_ROWS, :] = fold(jnp.concatenate([value, more], axis=0))
        tile[AT[2]:AT[2] + CORNER, :] = fold(last[TX - EDGE:])
        tile[AT[3]:AT[3] + CORNER, :] = fold(value[TX - EDGE:])
        tile[AT[4]:AT[4] + CORNER, :] = fold(last[0:EDGE])
        tile[AT[5]:AT[5] + CORNER, :] = fold(value[0:EDGE])
        tile[AT[6]:AT[6] + EDGE, :] = value[TX - EDGE:].astype(BF16)
        tile[AT[7]:AT[7] + EDGE, :] = value[0:EDGE].astype(BF16)

    def col_sum(ref):
        total = ref[pl.ds(0, CROW, stride=COARSE), :]
        for u in range(1, COARSE):
            total = total + ref[pl.ds(u, CROW, stride=COARSE), :]
        return total

    pick_row = iota((8, 128), 0)
    pick_cell = cell_of(iota((8, 128), 1))
    pick_in = iota((8, 128), 1) < TY
    pick_sum = jnp.where((pick_cell == pick_row) & pick_in, 1.0, 0.0)
    pick_dose = jnp.where((pick_cell == pick_row - 2) & pick_in, 1.0, 0.0)
    zs[...] = jnp.zeros_like(zs)
    sc[...] = jnp.zeros_like(sc)

    def sums_out(err_cols):
        parts = []
        for _ in range(3):
            parts.append(err_cols.astype(BF16).astype(F32))
            err_cols = err_cols - parts[-1]
        parts.append(jnp.zeros_like(err_cols))
        picks = jnp.concatenate([pick_sum, jnp.zeros_like(pick_sum)], axis=0).astype(BF16)
        sc[:, 0:32] = dot_nt(picks, jnp.concatenate(parts, axis=0).astype(BF16))
        got = sc[0:8, :]
        got = got + (pltpu.roll(got, 128 - CROW, 1) + pltpu.roll(got, 128 - 2 * CROW, 1))
        return pltpu.roll(jnp.where(lane < CROW, got, 0.0), s * CROW, 1)[0:4]

    def cells_out(cur_cols, spread):
        sc[8:16, 0:8] = dot_nt(pick_dose, cur_cols, HI)
        cells = pltpu.roll(jnp.where(lane < CROW, sc[8:16, :], 0.0), 64 + s * CROW, 1)
        cells = cells * (1.0 / (COARSE * COARSE))
        if spread is not None:
            zs[:, 0:8] = spread
            part = jnp.zeros((8, 128), F32)
            for d in range(5):
                part = part + pltpu.roll(zs[8 * d:8 * d + 8, :], 62 + d + s * CROW, 1)
            cells = cells - (STEP / (COARSE * COARSE)) * part
        return jnp.where(lane < 64, 0.0, cells)

    stage1, stage2 = (gs1, gd1), (gs2, gd2)

    def start_stage1(which, t, value):
        ref = stage1[which].at[t, own1]
        ref[...] = value
        for a, b in plane:
            pltpu.make_async_remote_copy(
                ref, ref, send_sem.at[which], recv_sem.at[t, which],
                device_id=(a, b), device_id_type=MESH,
            ).start()

    def start_stage2(which, t, value):
        ref = stage2[which].at[t, own2]
        ref[...] = value
        for a, b in column:
            pltpu.make_async_remote_copy(
                ref, ref, send_sem.at[2 + which], recv_sem.at[t, 2 + which],
                device_id=(a, b), device_id_type=MESH,
            ).start()

    def start_halo(t):
        sizes = (SIDE, SIDE, CORNER, CORNER, CORNER, CORNER, EDGE, EDGE)
        to = ((s, right), (s, left), (down, right), (down, left), (up, right), (up, left), (down, n), (up, n))
        for k in (2, 3, 4, 5, 6, 7, 0, 1):
            part = pl.ds(AT[k], sizes[k])
            pltpu.make_async_remote_copy(
                tile.at[part], halo.at[t, part], send_sem.at[4], recv_sem.at[t, 4],
                device_id=to[k], device_id_type=MESH,
            ).start()

    def all_of(ref, sem_send, sem_recv):
        return pltpu.make_async_remote_copy(
            ref, ref, sem_send, sem_recv, device_id=(s, right), device_id_type=MESH
        )

    def of_stage1(which, t):
        return all_of(stage1[which].at[t, pl.ds(0, 2 * ns - 1)], send_sem.at[which], recv_sem.at[t, which])

    def of_stage2(which, t):
        return all_of(stage2[which].at[t, pl.ds(0, nn // 2 - 1)], send_sem.at[2 + which], recv_sem.at[t, 2 + which])

    def of_halo(t):
        return all_of(halo.at[t], send_sem.at[4], recv_sem.at[t, 4])

    def assemble(t, centre):
        yes = lambda c: jnp.where(c, 1.0, 0.0).astype(F32)
        has_up, has_down = yes(s > 0), yes(s < ns - 1)
        has_left, has_right = yes(n > 0), yes(n < nn - 1)

        def band(row, rows, mid, lhs, rhs, flag):
            lhs = jnp.concatenate([pltpu.roll(lhs, 64, 1), lhs], axis=0)[0:rows] * (has_left * flag)
            rhs = jnp.concatenate([pltpu.roll(rhs, TY, 1), pltpu.roll(rhs, 36, 1)], axis=0)[0:rows] * (has_right * flag)
            et0[row:row + rows, :] = jnp.where(lane < TY, mid * flag, rhs)
            et1[row:row + rows, :] = jnp.where(lane < 32, rhs, jnp.where(lane >= 68, lhs, 0.0))

        def part(k, rows):
            return halo[t, pl.ds(AT[k], rows), :].astype(F32)

        band(0, EDGE, part(6, EDGE), part(2, CORNER), part(3, CORNER), has_up)
        band(EDGE, TX, centre, part(0, SIDE_ROWS), part(1, SIDE_ROWS), jnp.float32(1.0))
        band(EDGE + TX, EDGE, part(7, EDGE), part(4, CORNER), part(5, CORNER), has_down)

    def rows_result(which, t):
        totals = []
        for x in range(2):
            total = stage1[which][t, x * ns]
            for k in range(1, ns):
                total = total + stage1[which][t, x * ns + k]
            totals.append(total)
        total = jnp.concatenate(totals, axis=0)
        rows = total.shape[0]
        parts = []
        for _ in range(3):
            parts.append(total.astype(BF16).astype(F32))
            total = total - parts[-1]
        p = dot(jnp.concatenate(parts, axis=0).astype(BF16), mw[...])
        out = p[2 * rows:3 * rows, 0:128] + p[rows:2 * rows, 128:256] + p[0:rows, 256:384]
        out = out + p[rows:2 * rows, 0:128] + p[0:rows, 128:256]
        out = out + p[0:rows, 0:128]
        row = iota((rows, 128), 0)
        out = jnp.where(jnp.bitwise_and(row, 3) == iota((rows, 128), 1) // 32, out, 0.0)
        return jnp.concatenate(
            [jnp.sum(out[4 * k:4 * k + 4], axis=0, keepdims=True) for k in range(rows // 4)], axis=0)

    def turned_sums(t):
        stack = jnp.concatenate([gs2[t].reshape(nn, 128), jnp.zeros((128 - nn, 128), F32)], axis=0)
        turned = jnp.transpose(stack)
        out = turned[0:32]
        for k in range(1, 4):
            out = out + pltpu.roll(turned[32 * k:32 * k + 32], 32 * k, 1)
        return out

    def turned_cells(t):
        stack = jnp.concatenate([gd2[t].reshape(nn * 2, 128), jnp.zeros((64, 128), F32)], axis=0)
        turned = jnp.transpose(stack)
        return jnp.concatenate(
            [turned[0:32] + pltpu.roll(turned[32:64], 64, 1), turned[64:96] + pltpu.roll(turned[96:128], 64, 1)],
            axis=1)

    def dot_cols(lhs, table, first, last):
        rows = lhs.shape[0]
        parts = []
        for _ in range(3):
            parts.append(lhs.astype(BF16).astype(F32))
            lhs = lhs - parts[-1]
        p = dot(jnp.concatenate(parts, axis=0).astype(BF16), table[0, :, first:last])
        q2 = dot(jnp.concatenate(parts[0:2], axis=0).astype(BF16), table[1, :, first:last])
        q3 = dot(parts[0].astype(BF16), table[2, :, first:last])
        out = p[2 * rows:] + q2[rows:] + q3
        out = out + p[rows:2 * rows] + q2[0:rows]
        return out + p[0:rows]

    def set_back(t, from_sums):
        value = dot_cols(turned_cells(t)[24:32], td, 0, 128)
        value = BACK * (value if from_sums is None else value + from_sums)
        for u in range(COARSE):
            bk[pl.ds(u, CROW, stride=COARSE), :] = value

    def blur():
        for k in range(8):
            xb[:, 256 * k:256 * k + 128] = ct0[k + 2:k + 2 + BIN, :].astype(BF16)
            xb[:, 256 * k + 128:256 * k + 256] = ct1[k + 2:k + 2 + BIN, :].astype(BF16)
        blurred = None
        for pair in range(4):
            piece = dot(xb[...], wf[pair])
            lo = 16 * pair
            both = piece[lo:lo + TX, 0:128] + piece[lo + 8:lo + 8 + TX, 128:256]
            blurred = both if blurred is None else blurred + both
        bl[...] = blurred

    ps[...] = jnp.zeros_like(ps)
    ps[0:TAPS, 0:TAPS] = psf_ref[...].astype(F32)
    taps = ps[...]
    taps_h = taps.astype(BF16)
    b_at, l_at = iota((128, 128), 0), iota((128, 128), 1)
    perm_f = jnp.where((l_at == lax.rem(RIM - b_at + 256, 128)) & (b_at < TAPS), 1.0, 0.0).astype(BF16)
    perm_a = jnp.where((l_at == lax.rem(b_at - RIM + 256, 128)) & (b_at < TAPS), 1.0, 0.0).astype(BF16)
    flip = jnp.where(iota((64, 64), 1) == TAPS - 1 - iota((64, 64), 0), 1.0, 0.0).astype(BF16)
    rf[...] = dot(taps_h, perm_f)
    ra[...] = dot(dot(flip, taps_h).astype(BF16), perm_a)

    dose = jnp.zeros((TX, 128), F32)
    own[0:TX, :] = dose
    own[0:TX, 0:TY] = dose_ref[...].astype(F32)
    tile[...] = jnp.zeros_like(tile)
    field_out(own[0:TX, :])
    first_payload = cells_out(col_sum(own), None)

    g_row = jnp.bitwise_and(b_at, 63)
    l32 = jnp.bitwise_and(l_at, 31)
    full_rows = gauss(iota((ncx, ncx), 0) - iota((ncx, ncx), 1))
    l64 = jnp.bitwise_and(iota((ncx, 128), 1), 31)
    twice = dot(full_rows, gauss(iota((ncx, 128), 0) - (s * CROW + l64 - 16)), HI)
    upper = jnp.concatenate([twice, jnp.zeros((128 - ncx, 128), F32)], axis=0)
    low = b_at < 64
    table = jnp.where(low & (l32 < 12), gauss(g_row - (s * CROW + l32 - 2)), 0.0)
    table = table + jnp.where(low & (l32 >= 16) & (l32 < 24), upper, 0.0)
    table = table + jnp.where((~low) & (l32 >= 24), gauss(g_row - (s * CROW + l32 - 24)), 0.0)
    table = jnp.where(g_row < ncx, table, 0.0)
    for k in range(3):
        rounded = table.astype(BF16)
        mw[:, 128 * k:128 * k + 128] = rounded
        table = table - rounded.astype(F32)
    mw[:, 384:512] = jnp.zeros((128, 128), BF16)

    k_at, a_at = iota((128, 64), 0), iota((128, 64), 1)
    u_at = k_at // 5
    low_a = COARSE * (k_at - 5 * u_at - 2) - u_at + RIM
    rows_w = jnp.where((a_at >= low_a) & (a_at < low_a + COARSE), 1.0, 0.0).astype(BF16)
    x_at = -2 * COARSE - jnp.where(l_at < 16, l_at, l_at - 128)
    cols_w = jnp.where((b_at >= x_at + RIM) & (b_at < x_at + RIM + COARSE), 1.0, 0.0)
    fr[...] = dot(dot(rows_w, taps_h), cols_w, HI)
    j8 = iota((8, 128), 0)
    c8 = iota((8, 128), 1)
    xx = COARSE * (j8 - 2) - c8
    inside = (xx >= RIM - 84) & (xx <= RIM) & (c8 < TY)
    for u in range(COARSE):
        pieces = []
        for d in range(5):
            row = jnp.broadcast_to(fr[5 * u + d:5 * u + d + 1, :], (8, 128))
            row = pltpu.roll(pltpu.roll(row, 0, 1, stride=12, stride_axis=0), 0, 1, stride=13, stride_axis=0)
            pieces.append(jnp.where(inside, row, 0.0))
        for d in range(5):
            top = pieces[d].astype(BF16).astype(F32)
            both = jnp.concatenate([top, pieces[d] - top], axis=0).astype(BF16)
            vv[16 * d:16 * d + 16, 128 * u:128 * u + 128] = both

    pl.semaphore_wait(barrier, len(plane) + len(column) + 6)
    start_stage1(1, 0, first_payload)
    start_halo(0)

    near = jnp.abs(b_at - l_at) <= RIM

    def circulant(row):
        full = pltpu.roll(jnp.broadcast_to(row, (128, 128)), 0, 1, stride=1, stride_axis=0)
        return jnp.where(near, full, 0.0).astype(BF16), jnp.where(near, 0.0, full).astype(BF16)

    def one_pair(k, carry):
        pair, shift = k // 8, lax.rem(k, 8)
        at_row = pl.multiple_of(shift * 256, 256)
        for half in range(2):
            tap = pair * 16 + half * 8 + shift
            same, other = circulant(rf[pl.ds(tap, 1), :])
            wf[pair, pl.ds(at_row, 128), half * 128:half * 128 + 128] = same
            wf[pair, pl.ds(at_row + 128, 128), half * 128:half * 128 + 128] = other
            same, other = circulant(ra[pl.ds(tap, 1), :])
            group = pair * 2 + half
            wa[group, pl.ds(at_row, 128), 0:128] = same
            wa[group, pl.ds(at_row, 128), 128:256] = other
            wa[group, pl.ds(at_row + 128, 128), 0:128] = other
            wa[group, pl.ds(at_row + 128, 128), 128:256] = same
        return carry

    lax.fori_loop(0, 32, one_pair, 0)

    of_stage1(1, 0).wait_recv()
    start_stage2(1, 0, rows_result(1, 0))

    def split(table, first, value):
        for k in range(3):
            rounded = value.astype(BF16)
            table[k, :, first:first + value.shape[1]] = rounded
            value = value - rounded.astype(F32)

    def sum_col(width):
        at = iota((nn * 4, width), 0)
        z, c, x = jnp.bitwise_and(at, 31) // 4, jnp.bitwise_and(at // 2, 1), jnp.bitwise_and(at, 1)
        return CCOL * (4 * z + 2 * x + c) + at // 32

    pos = iota((nn * 4, 256), 1)
    col = jnp.where(pos < 160, pos, pos - 256)
    split(ts, 0, gauss(sum_col(256) - (CCOL * n + cell_of(col))))
    mid = gauss(iota((ncy, 128), 0) - (CCOL * n + cell_of(iota((ncy, 128), 1))))
    outer = gauss(sum_col(ncy) - iota((nn * 4, ncy), 1))
    split(ts, 256, (-STEP * ADJ_SCALE) * dot(outer, mid, HI))
    at = iota((nn * 8, 128), 0)
    pos = jnp.bitwise_and(at, 63)
    z, c, x = pos // 8, jnp.bitwise_and(pos // 4, 1), jnp.bitwise_and(pos // 2, 1)
    at = CCOL * (4 * z + 2 * x + c) + 4 * jnp.bitwise_and(at, 1) + at // 64 - 2
    lane_cell = CCOL * n + cell_of(iota((nn * 8, 128), 1))
    split(td, 0, jnp.where((at >= 0) & (at < ncy), gauss(at - lane_cell), 0.0))


    et0[AIN + 8:, :] = jnp.zeros((EROWS - AIN - 8, 128), F32)
    et1[AIN + 8:, :] = jnp.zeros((EROWS - AIN - 8, 128), F32)
    ct0[AOUT:, :] = jnp.zeros((CROWS - AOUT, 128), F32)
    ct1[AOUT:, :] = jnp.zeros((CROWS - AOUT, 128), F32)

    of_halo(0).wait_recv()
    assemble(0, own[0:TX, :])
    ct0[0:AOUT, :] = et0[32:32 + AOUT, :]
    ct1[0:AOUT, :] = et1[32:32 + AOUT, :]

    blur()
    of_stage2(1, 0).wait_recv()
    set_back(0, None)
    of_stage1(1, 0).wait_send()
    of_stage2(1, 0).wait_send()
    of_halo(0).wait_send()

    yes = lambda c: jnp.where(c, 1.0, 0.0).astype(F32)
    row_ok = jnp.ones((AOUT, 1), F32)
    r_at = iota((AOUT, 1), 0) - 32
    row_ok = jnp.where(r_at < 0, yes(s > 0), jnp.where(r_at >= TX, yes(s < ns - 1), 1.0))
    mask0 = jnp.where(lane < TY, 1.0, yes(n < nn - 1))
    mask1 = jnp.where(lane < 32, yes(n < nn - 1), yes(n > 0))

    def iteration(t, carry):
        exposure = bl[...] + bk[0:TX, :]
        resist = jax.nn.sigmoid(GAIN * (exposure - LEVEL))
        own[0:TX, 0:TY] = target_ref[...].astype(F32)
        error = (resist - own[0:TX, :]) * GAIN * resist * (1.0 - resist)
        error = jnp.where(lane < TY, error, 0.0)
        err[0:TX, :] = error
        half = error.astype(BF16).astype(F32)
        own[0:TX, :] = half
        field_out(half)
        both_ref[0:TX, :] = resist[:, 0:TY]

        start_stage1(0, t, sums_out(col_sum(err)))
        @pl.when(t < ITERS)
        def _():
            cells_in = jnp.concatenate(
                [own[pl.ds(u, CROW, stride=COARSE), :].astype(BF16) for u in range(COARSE)], axis=1)
            two = dot_nt(vv[...], cells_in)
            spread = jnp.concatenate([two[16 * d:16 * d + 8] + two[16 * d + 8:16 * d + 16] for d in range(5)], axis=0)
            cur_cols = jnp.where(lane < TY, col_sum(ct0.at[pl.ds(32, TX)]), 0.0)
            start_stage1(1, t, cells_out(cur_cols, spread))

        start_halo(t)

        of_stage1(0, t).wait_recv()
        start_stage2(0, t, rows_result(0, t))

        @pl.when(t < ITERS)
        def _():
            of_stage1(1, t).wait_recv()
            start_stage2(1, t, rows_result(1, t))

        of_halo(t).wait_recv()
        assemble(t, own[0:TX, :])
        for k in range(8):
            xa[:, 256 * k:256 * k + 128] = et0[k + 2:k + 2 + AIN, :].astype(BF16)
            xa[:, 256 * k + 128:256 * k + 256] = et1[k + 2:k + 2 + AIN, :].astype(BF16)
        for group in range(8):
            piece = dot(xa[...], wa[group])
            lo = 8 * group
            if group == 0:
                at0[...] = piece[lo:lo + AOUT, 0:128]
                at1[...] = piece[lo:lo + AOUT, 128:256]
            else:
                at0[...] += piece[lo:lo + AOUT, 0:128]
                at1[...] += piece[lo:lo + AOUT, 128:256]

        of_stage2(0, t).wait_recv()
        turned = turned_sums(t)
        out = dot_cols(turned[0:16], ts, 0, 256)
        for u in range(COARSE):
            for ref, first in ((ub0, 0), (ub1, 128)):
                ref[pl.ds(6 + u, 8, stride=COARSE), :] = out[0:8, first:first + 128]
                ref[pl.ds(206 + u, 8, stride=COARSE), :] = out[8:16, first:first + 128]
        new0 = ct0[0:AOUT, :] - STEP * (at0[...] + ADJ_SCALE * ub0[24:24 + AOUT, :])
        new1 = ct1[0:AOUT, :] - STEP * (at1[...] + ADJ_SCALE * ub1[24:24 + AOUT, :])
        both_ref[TX:, :] = new0[32:32 + TX, 0:TY]
        ct0[0:AOUT, :] = new0.astype(BF16).astype(F32) * (row_ok * mask0)
        ct1[0:AOUT, :] = new1.astype(BF16).astype(F32) * (row_ok * mask1)

        @pl.when(t < ITERS)
        def _():
            blur()
            from_sums = dot_cols(turned[16:24], ts, 256, 384)
            of_stage2(1, t).wait_recv()
            set_back(t, from_sums)
            of_stage1(1, t).wait_send()
            of_stage2(1, t).wait_send()

        of_stage1(0, t).wait_send()
        of_stage2(0, t).wait_send()
        of_halo(t).wait_send()
        return carry

    lax.fori_loop(1, PHASES, iteration, 0)


def solution(mesh):
    ns, nn = mesh.shape["stripe"], mesh.shape["scan"]

    def per_device(dose, target, psf):
        vmem = pl.BlockSpec(memory_space=pltpu.VMEM)
        f = lambda *shape: pltpu.VMEM(shape, F32)
        h = lambda *shape: pltpu.VMEM(shape, BF16)
        both = pl.pallas_call(
            lambda *refs: kernel(ns, nn, *refs),
            out_shape=jax.ShapeDtypeStruct((2 * TX, TY), F32),
            in_specs=[vmem] * 3,
            out_specs=vmem,
            scratch_shapes=[
                f(PHASES, 2 * ns, 4, 128), f(PHASES, 2 * ns, 8, 128),
                f(PHASES, nn // 2, 2, 128), f(PHASES, nn // 2, 4, 128), h(PHASES, HALO, 128),
                h(HALO, 128),
                f(EROWS, 128), f(EROWS, 128), f(CROWS, 128), f(CROWS, 128),
                f(AOUT, 128), f(AOUT, 128),
                h(8, 2048, 256), h(4, 2048, 256), h(80, 3200),
                f(64, 128), f(64, 128), f(64, 128), f(128, 128),
                h(AIN, 2048), h(BIN, 2048),
                f(232, 128), f(232, 128), f(40, 128), f(16, 128),
                h(128, 512), h(3, nn * 4, 384), h(3, nn * 8, 128), f(448, 128), f(448, 128), f(232, 128), f(TX, 128),
                pltpu.SemaphoreType.DMA((5,)), pltpu.SemaphoreType.DMA((PHASES, 5)),
            ],
            compiler_params=pltpu.CompilerParams(
                collective_id=0, has_side_effects=True, vmem_limit_bytes=60 << 20
            ),
            name="dose",
        )(dose, target, psf)
        return both[0:TX], both[TX:]

    return jax.shard_map(
        per_device, mesh=mesh,
        in_specs=(P("stripe", "scan"), P("stripe", "scan"), P()),
        out_specs=(P("stripe", "scan"), P("stripe", "scan")),
        check_vma=False,
    )
```

```python
import math

import jax
import jax.numpy as jnp
from jax import lax
from jax.experimental import pallas as pl
from jax.experimental.pallas import tpu as pltpu
from jax.sharding import PartitionSpec as P

TX, TY = 200, 100
TAPS = 61
COARSE = 25
SIGMA = 40
ITERS = 4
RIM = 30
BACK = 0.6
GAIN = 3.0
LEVEL = 1.5
STEP = 0.5
CROW, CCOL = TX // COARSE, TY // COARSE
ADJ_SCALE = BACK / (COARSE * COARSE)

MESH = pl.DeviceIdType.MESH
F32, BF16 = jnp.float32, jnp.bfloat16
HI = lax.Precision.HIGHEST

EROWS = 336
CROWS = 272
AOUT = 264
AIN = 320
BIN = 256
PHASES = ITERS + 1
SIDE = 112
SIDE_ROWS = 104
CORNER = 32
EDGE = 64
AT = (0, SIDE, 2 * SIDE, 2 * SIDE + CORNER, 2 * SIDE + 2 * CORNER, 2 * SIDE + 3 * CORNER,
      2 * SIDE + 4 * CORNER, 2 * SIDE + 4 * CORNER + EDGE)
HALO = 2 * SIDE + 4 * CORNER + 2 * EDGE


def iota(shape, dim):
    return lax.broadcasted_iota(jnp.int32, shape, dim)


def dot(a, b, precision=None):
    return jnp.dot(a, b, precision=precision, preferred_element_type=F32)


def dot_nt(a, b, precision=None):
    return lax.dot_general(
        a, b, (((1,), (1,)), ((), ())), precision=precision, preferred_element_type=F32
    )


def gauss(dist):
    d = dist.astype(F32)
    return jnp.exp(-d * d / (2.0 * SIGMA * SIGMA)) / (math.sqrt(2.0 * math.pi) * SIGMA)


def cell_of(col):
    out = jnp.full(col.shape, -3, jnp.int32)
    for k in range(-2, 7):
        out = out + jnp.where(col >= COARSE * k, 1, 0)
    return out


def kernel(
    ns, nn, dose_hbm, target_hbm, psf_hbm, both_hbm, dose_ref, target_ref, psf_ref, both_ref,
    gs1, gd1, gs2, gd2, halo, tile, et0, et1, ct0, ct1, at0, at1, wa, wf, vv,
    ps, rf, ra, fr, xa, xb, err, own, zs, sc, mw, ts, td, ub0, ub1, bk, bl,
    send_sem, recv_sem, local_sem,
):
    s = lax.axis_index("stripe")
    n = lax.axis_index("scan")
    ncx, ncy = ns * CROW, nn * CCOL
    up, down = lax.rem(s + ns - 1, ns), lax.rem(s + 1, ns)
    left, right = lax.rem(n + nn - 1, nn), lax.rem(n + 1, nn)

    x_lo = lax.rem(n // 2, 2)
    core = lax.rem(n, 2)
    far = lambda count: sorted(range(count), key=lambda k: -min(k, count - k))
    plane, column = [], []
    for k in far(ns):
        for flip in (1, 0):
            if k or flip:
                plane.append((lax.rem(s + k, ns), n + 2 * flip * (1 - 2 * x_lo)))
    for k in far(nn // 4):
        for flip in (1, 0):
            if k or flip:
                column.append((s, lax.rem(n + 4 * k, nn) + flip * (1 - 2 * core)))
    own1, own2 = x_lo * ns + s, (n // 4) * 2 + core
    barrier = pltpu.get_barrier_semaphore()

    def hello(a, b):
        pl.semaphore_signal(barrier, inc=1, device_id=(a, b), device_id_type=MESH)

    for a in (up, down):
        for b in (left, right):
            hello(a, b)
    for b in (left, right):
        hello(s, b)
    for a, b in plane + column:
        hello(a, b)

    get_dose = pltpu.make_async_copy(dose_hbm, dose_ref, local_sem.at[0])
    get_psf = pltpu.make_async_copy(psf_hbm, psf_ref, local_sem.at[1])
    get_target = pltpu.make_async_copy(target_hbm, target_ref, local_sem.at[2])
    get_dose.start()
    get_psf.start()
    get_target.start()
    put_resist = pltpu.make_async_copy(both_ref.at[pl.ds(0, TX)], both_hbm.at[pl.ds(0, TX)], local_sem.at[3])
    put_dose = pltpu.make_async_copy(both_ref.at[pl.ds(TX, TX)], both_hbm.at[pl.ds(TX, TX)], local_sem.at[4])

    lane = iota((1, 128), 1)

    def fold(value):
        half = value.shape[0] // 2
        return jnp.where(lane < 64, value[0:half], pltpu.roll(value[half:], 64, 1)).astype(BF16)

    def field_out(value):
        last = pltpu.roll(value, 92, 1)
        more = jnp.zeros((2 * SIDE_ROWS - TX, 128), F32)
        tile[AT[0]:AT[0] + SIDE_ROWS, :] = fold(jnp.concatenate([last, more], axis=0))
        tile[AT[1]:AT[1] + SIDE_ROWS, :] = fold(jnp.concatenate([value, more], axis=0))
        tile[AT[2]:AT[2] + CORNER, :] = fold(last[TX - EDGE:])
        tile[AT[3]:AT[3] + CORNER, :] = fold(value[TX - EDGE:])
        tile[AT[4]:AT[4] + CORNER, :] = fold(last[0:EDGE])
        tile[AT[5]:AT[5] + CORNER, :] = fold(value[0:EDGE])
        tile[AT[6]:AT[6] + EDGE, :] = value[TX - EDGE:].astype(BF16)
        tile[AT[7]:AT[7] + EDGE, :] = value[0:EDGE].astype(BF16)

    def col_sum(ref):
        total = ref[pl.ds(0, CROW, stride=COARSE), :]
        for u in range(1, COARSE):
            total = total + ref[pl.ds(u, CROW, stride=COARSE), :]
        return total

    pick_row = iota((8, 128), 0)
    pick_cell = cell_of(iota((8, 128), 1))
    pick_in = iota((8, 128), 1) < TY
    pick_sum = jnp.where((pick_cell == pick_row) & pick_in, 1.0, 0.0)
    pick_dose = jnp.where((pick_cell == pick_row - 2) & pick_in, 1.0, 0.0)
    zs[...] = jnp.zeros_like(zs)
    sc[...] = jnp.zeros_like(sc)

    def sums_out(err_cols):
        parts = []
        for _ in range(3):
            parts.append(err_cols.astype(BF16).astype(F32))
            err_cols = err_cols - parts[-1]
        parts.append(jnp.zeros_like(err_cols))
        picks = jnp.concatenate([pick_sum, jnp.zeros_like(pick_sum)], axis=0).astype(BF16)
        sc[:, 0:32] = dot_nt(picks, jnp.concatenate(parts, axis=0).astype(BF16))
        got = sc[0:8, :]
        got = got + (pltpu.roll(got, 128 - CROW, 1) + pltpu.roll(got, 128 - 2 * CROW, 1))
        return pltpu.roll(jnp.where(lane < CROW, got, 0.0), s * CROW, 1)[0:4]

    def cells_out(cur_cols, spread):
        sc[8:16, 0:8] = dot_nt(pick_dose, cur_cols, HI)
        cells = pltpu.roll(jnp.where(lane < CROW, sc[8:16, :], 0.0), 64 + s * CROW, 1)
        cells = cells * (1.0 / (COARSE * COARSE))
        if spread is not None:
            zs[:, 0:8] = spread
            part = jnp.zeros((8, 128), F32)
            for d in range(5):
                part = part + pltpu.roll(zs[8 * d:8 * d + 8, :], 62 + d + s * CROW, 1)
            cells = cells - (STEP / (COARSE * COARSE)) * part
        return jnp.where(lane < 64, 0.0, cells)

    stage1, stage2 = (gs1, gd1), (gs2, gd2)

    def start_stage1(which, t, value):
        ref = stage1[which].at[t, own1]
        ref[...] = value
        for a, b in plane:
            pltpu.make_async_remote_copy(
                ref, ref, send_sem.at[which], recv_sem.at[t, which],
                device_id=(a, b), device_id_type=MESH,
            ).start()

    def start_stage2(which, t, value):
        ref = stage2[which].at[t, own2]
        ref[...] = value
        for a, b in column:
            pltpu.make_async_remote_copy(
                ref, ref, send_sem.at[2 + which], recv_sem.at[t, 2 + which],
                device_id=(a, b), device_id_type=MESH,
            ).start()

    def start_halo(t):
        sizes = (SIDE, SIDE, CORNER, CORNER, CORNER, CORNER, EDGE, EDGE)
        to = ((s, right), (s, left), (down, right), (down, left), (up, right), (up, left), (down, n), (up, n))
        for k in (2, 3, 4, 5, 6, 7, 0, 1):
            part = pl.ds(AT[k], sizes[k])
            pltpu.make_async_remote_copy(
                tile.at[part], halo.at[t, part], send_sem.at[4], recv_sem.at[t, 4],
                device_id=to[k], device_id_type=MESH,
            ).start()

    def all_of(ref, sem_send, sem_recv):
        return pltpu.make_async_remote_copy(
            ref, ref, sem_send, sem_recv, device_id=(s, right), device_id_type=MESH
        )

    def of_stage1(which, t):
        return all_of(stage1[which].at[t, pl.ds(0, 2 * ns - 1)], send_sem.at[which], recv_sem.at[t, which])

    def of_stage2(which, t):
        return all_of(stage2[which].at[t, pl.ds(0, nn // 2 - 1)], send_sem.at[2 + which], recv_sem.at[t, 2 + which])

    def of_halo(t):
        return all_of(halo.at[t], send_sem.at[4], recv_sem.at[t, 4])

    def assemble(t, centre):
        yes = lambda c: jnp.where(c, 1.0, 0.0).astype(F32)
        has_up, has_down = yes(s > 0), yes(s < ns - 1)
        has_left, has_right = yes(n > 0), yes(n < nn - 1)

        def band(row, rows, mid, lhs, rhs, flag):
            lhs = jnp.concatenate([pltpu.roll(lhs, 64, 1), lhs], axis=0)[0:rows] * (has_left * flag)
            rhs = jnp.concatenate([pltpu.roll(rhs, TY, 1), pltpu.roll(rhs, 36, 1)], axis=0)[0:rows] * (has_right * flag)
            et0[row:row + rows, :] = jnp.where(lane < TY, mid * flag, rhs)
            et1[row:row + rows, :] = jnp.where(lane < 32, rhs, jnp.where(lane >= 68, lhs, 0.0))

        def part(k, rows):
            return halo[t, pl.ds(AT[k], rows), :].astype(F32)

        band(0, EDGE, part(6, EDGE), part(2, CORNER), part(3, CORNER), has_up)
        band(EDGE, TX, centre, part(0, SIDE_ROWS), part(1, SIDE_ROWS), jnp.float32(1.0))
        band(EDGE + TX, EDGE, part(7, EDGE), part(4, CORNER), part(5, CORNER), has_down)

    def rows_result(which, t):
        totals = []
        for x in range(2):
            total = stage1[which][t, x * ns]
            for k in range(1, ns):
                total = total + stage1[which][t, x * ns + k]
            totals.append(total)
        total = jnp.concatenate(totals, axis=0)
        rows = total.shape[0]
        parts = []
        for _ in range(3):
            parts.append(total.astype(BF16).astype(F32))
            total = total - parts[-1]
        p = dot(jnp.concatenate(parts, axis=0).astype(BF16), mw[...])
        out = p[2 * rows:3 * rows, 0:128] + p[rows:2 * rows, 128:256] + p[0:rows, 256:384]
        out = out + p[rows:2 * rows, 0:128] + p[0:rows, 128:256]
        out = out + p[0:rows, 0:128]
        row = iota((rows, 128), 0)
        out = jnp.where(jnp.bitwise_and(row, 3) == iota((rows, 128), 1) // 32, out, 0.0)
        return jnp.concatenate(
            [jnp.sum(out[4 * k:4 * k + 4], axis=0, keepdims=True) for k in range(rows // 4)], axis=0)

    def turned_sums(t):
        stack = jnp.concatenate([gs2[t].reshape(nn, 128), jnp.zeros((128 - nn, 128), F32)], axis=0)
        turned = jnp.transpose(stack)
        out = turned[0:32]
        for k in range(1, 4):
            out = out + pltpu.roll(turned[32 * k:32 * k + 32], 32 * k, 1)
        return out

    def turned_cells(t):
        stack = jnp.concatenate([gd2[t].reshape(nn * 2, 128), jnp.zeros((64, 128), F32)], axis=0)
        turned = jnp.transpose(stack)
        return jnp.concatenate(
            [turned[0:32] + pltpu.roll(turned[32:64], 64, 1), turned[64:96] + pltpu.roll(turned[96:128], 64, 1)],
            axis=1)

    def dot_cols(lhs, table, first, last):
        rows = lhs.shape[0]
        parts = []
        for _ in range(3):
            parts.append(lhs.astype(BF16).astype(F32))
            lhs = lhs - parts[-1]
        p = dot(jnp.concatenate(parts, axis=0).astype(BF16), table[0, :, first:last])
        q2 = dot(jnp.concatenate(parts[0:2], axis=0).astype(BF16), table[1, :, first:last])
        q3 = dot(parts[0].astype(BF16), table[2, :, first:last])
        out = p[2 * rows:] + q2[rows:] + q3
        out = out + p[rows:2 * rows] + q2[0:rows]
        return out + p[0:rows]

    def set_back(t, from_sums):
        value = dot_cols(turned_cells(t)[24:32], td, 0, 128)
        value = BACK * (value if from_sums is None else value + from_sums)
        for u in range(COARSE):
            bk[pl.ds(u, CROW, stride=COARSE), :] = value

    def blur():
        for k in range(8):
            xb[:, 256 * k:256 * k + 128] = ct0[k + 2:k + 2 + BIN, :].astype(BF16)
            xb[:, 256 * k + 128:256 * k + 256] = ct1[k + 2:k + 2 + BIN, :].astype(BF16)
        blurred = None
        for pair in range(4):
            piece = dot(xb[...], wf[pair])
            lo = 16 * pair
            both = piece[lo:lo + TX, 0:128] + piece[lo + 8:lo + 8 + TX, 128:256]
            blurred = both if blurred is None else blurred + both
        bl[...] = blurred

    get_dose.wait()
    dose = jnp.zeros((TX, 128), F32)
    own[0:TX, :] = dose
    own[0:TX, 0:TY] = dose_ref[...].astype(F32)
    tile[...] = jnp.zeros_like(tile)
    field_out(own[0:TX, :])
    first_payload = cells_out(col_sum(own), None)

    ps[...] = jnp.zeros_like(ps)
    get_psf.wait()
    ps[0:TAPS, 0:TAPS] = psf_ref[...].astype(F32)
    taps = ps[...]
    taps_h = taps.astype(BF16)
    b_at, l_at = iota((128, 128), 0), iota((128, 128), 1)
    perm_f = jnp.where((l_at == lax.rem(RIM - b_at + 256, 128)) & (b_at < TAPS), 1.0, 0.0).astype(BF16)
    perm_a = jnp.where((l_at == lax.rem(b_at - RIM + 256, 128)) & (b_at < TAPS), 1.0, 0.0).astype(BF16)
    flip = jnp.where(iota((64, 64), 1) == TAPS - 1 - iota((64, 64), 0), 1.0, 0.0).astype(BF16)
    rf[...] = dot(taps_h, perm_f)
    ra[...] = dot(dot(flip, taps_h).astype(BF16), perm_a)

    g_row = jnp.bitwise_and(b_at, 63)
    l32 = jnp.bitwise_and(l_at, 31)
    full_rows = gauss(iota((ncx, ncx), 0) - iota((ncx, ncx), 1))
    l64 = jnp.bitwise_and(iota((ncx, 128), 1), 31)
    twice = dot(full_rows, gauss(iota((ncx, 128), 0) - (s * CROW + l64 - 16)), HI)
    upper = jnp.concatenate([twice, jnp.zeros((128 - ncx, 128), F32)], axis=0)
    low = b_at < 64
    table = jnp.where(low & (l32 < 12), gauss(g_row - (s * CROW + l32 - 2)), 0.0)
    table = table + jnp.where(low & (l32 >= 16) & (l32 < 24), upper, 0.0)
    table = table + jnp.where((~low) & (l32 >= 24), gauss(g_row - (s * CROW + l32 - 24)), 0.0)
    table = jnp.where(g_row < ncx, table, 0.0)
    for k in range(3):
        rounded = table.astype(BF16)
        mw[:, 128 * k:128 * k + 128] = rounded
        table = table - rounded.astype(F32)
    mw[:, 384:512] = jnp.zeros((128, 128), BF16)

    k_at, a_at = iota((128, 64), 0), iota((128, 64), 1)
    u_at = k_at // 5
    low_a = COARSE * (k_at - 5 * u_at - 2) - u_at + RIM
    rows_w = jnp.where((a_at >= low_a) & (a_at < low_a + COARSE), 1.0, 0.0).astype(BF16)
    x_at = -2 * COARSE - jnp.where(l_at < 16, l_at, l_at - 128)
    cols_w = jnp.where((b_at >= x_at + RIM) & (b_at < x_at + RIM + COARSE), 1.0, 0.0)
    fr[...] = dot(dot(rows_w, taps_h), cols_w, HI)
    j8 = iota((8, 128), 0)
    c8 = iota((8, 128), 1)
    xx = COARSE * (j8 - 2) - c8
    inside = (xx >= RIM - 84) & (xx <= RIM) & (c8 < TY)
    for u in range(COARSE):
        pieces = []
        for d in range(5):
            row = jnp.broadcast_to(fr[5 * u + d:5 * u + d + 1, :], (8, 128))
            row = pltpu.roll(pltpu.roll(row, 0, 1, stride=12, stride_axis=0), 0, 1, stride=13, stride_axis=0)
            pieces.append(jnp.where(inside, row, 0.0))
        for d in range(5):
            top = pieces[d].astype(BF16).astype(F32)
            both = jnp.concatenate([top, pieces[d] - top], axis=0).astype(BF16)
            vv[16 * d:16 * d + 16, 128 * u:128 * u + 128] = both

    pl.semaphore_wait(barrier, len(plane) + len(column) + 6)
    start_stage1(1, 0, first_payload)
    start_halo(0)

    near = jnp.abs(b_at - l_at) <= RIM

    def circulant(row):
        full = pltpu.roll(jnp.broadcast_to(row, (128, 128)), 0, 1, stride=1, stride_axis=0)
        return jnp.where(near, full, 0.0).astype(BF16), jnp.where(near, 0.0, full).astype(BF16)

    def one_pair(k, carry):
        pair, shift = k // 8, lax.rem(k, 8)
        at_row = pl.multiple_of(shift * 256, 256)
        for half in range(2):
            tap = pair * 16 + half * 8 + shift
            same, other = circulant(rf[pl.ds(tap, 1), :])
            wf[pair, pl.ds(at_row, 128), half * 128:half * 128 + 128] = same
            wf[pair, pl.ds(at_row + 128, 128), half * 128:half * 128 + 128] = other
            same, other = circulant(ra[pl.ds(tap, 1), :])
            group = pair * 2 + half
            wa[group, pl.ds(at_row, 128), 0:128] = same
            wa[group, pl.ds(at_row, 128), 128:256] = other
            wa[group, pl.ds(at_row + 128, 128), 0:128] = other
            wa[group, pl.ds(at_row + 128, 128), 128:256] = same
        return carry

    lax.fori_loop(0, 32, one_pair, 0)

    of_stage1(1, 0).wait_recv()
    start_stage2(1, 0, rows_result(1, 0))

    def split(table, first, value):
        for k in range(3):
            rounded = value.astype(BF16)
            table[k, :, first:first + value.shape[1]] = rounded
            value = value - rounded.astype(F32)

    def sum_col(width):
        at = iota((nn * 4, width), 0)
        z, c, x = jnp.bitwise_and(at, 31) // 4, jnp.bitwise_and(at // 2, 1), jnp.bitwise_and(at, 1)
        return CCOL * (4 * z + 2 * x + c) + at // 32

    pos = iota((nn * 4, 256), 1)
    col = jnp.where(pos < 160, pos, pos - 256)
    split(ts, 0, gauss(sum_col(256) - (CCOL * n + cell_of(col))))
    mid = gauss(iota((ncy, 128), 0) - (CCOL * n + cell_of(iota((ncy, 128), 1))))
    outer = gauss(sum_col(ncy) - iota((nn * 4, ncy), 1))
    split(ts, 256, (-STEP * ADJ_SCALE) * dot(outer, mid, HI))
    at = iota((nn * 8, 128), 0)
    pos = jnp.bitwise_and(at, 63)
    z, c, x = pos // 8, jnp.bitwise_and(pos // 4, 1), jnp.bitwise_and(pos // 2, 1)
    at = CCOL * (4 * z + 2 * x + c) + 4 * jnp.bitwise_and(at, 1) + at // 64 - 2
    lane_cell = CCOL * n + cell_of(iota((nn * 8, 128), 1))
    split(td, 0, jnp.where((at >= 0) & (at < ncy), gauss(at - lane_cell), 0.0))


    et0[AIN + 8:, :] = jnp.zeros((EROWS - AIN - 8, 128), F32)
    et1[AIN + 8:, :] = jnp.zeros((EROWS - AIN - 8, 128), F32)
    ct0[AOUT:, :] = jnp.zeros((CROWS - AOUT, 128), F32)
    ct1[AOUT:, :] = jnp.zeros((CROWS - AOUT, 128), F32)

    of_halo(0).wait_recv()
    assemble(0, own[0:TX, :])
    ct0[0:AOUT, :] = et0[32:32 + AOUT, :]
    ct1[0:AOUT, :] = et1[32:32 + AOUT, :]

    blur()
    of_stage2(1, 0).wait_recv()
    set_back(0, None)
    of_stage1(1, 0).wait_send()
    of_stage2(1, 0).wait_send()
    of_halo(0).wait_send()

    yes = lambda c: jnp.where(c, 1.0, 0.0).astype(F32)
    row_ok = jnp.ones((AOUT, 1), F32)
    r_at = iota((AOUT, 1), 0) - 32
    row_ok = jnp.where(r_at < 0, yes(s > 0), jnp.where(r_at >= TX, yes(s < ns - 1), 1.0))
    mask0 = jnp.where(lane < TY, 1.0, yes(n < nn - 1))
    mask1 = jnp.where(lane < 32, yes(n < nn - 1), yes(n > 0))

    get_target.wait()

    def iteration(t, carry):
        exposure = bl[...] + bk[0:TX, :]
        resist = jax.nn.sigmoid(GAIN * (exposure - LEVEL))
        own[0:TX, 0:TY] = target_ref[...].astype(F32)
        error = (resist - own[0:TX, :]) * GAIN * resist * (1.0 - resist)
        error = jnp.where(lane < TY, error, 0.0)
        err[0:TX, :] = error
        half = error.astype(BF16).astype(F32)
        own[0:TX, :] = half
        field_out(half)
        both_ref[0:TX, :] = resist[:, 0:TY]

        @pl.when(t == ITERS)
        def _():
            put_resist.start()


        start_stage1(0, t, sums_out(col_sum(err)))
        @pl.when(t < ITERS)
        def _():
            cells_in = jnp.concatenate(
                [own[pl.ds(u, CROW, stride=COARSE), :].astype(BF16) for u in range(COARSE)], axis=1)
            two = dot_nt(vv[...], cells_in)
            spread = jnp.concatenate([two[16 * d:16 * d + 8] + two[16 * d + 8:16 * d + 16] for d in range(5)], axis=0)
            cur_cols = jnp.where(lane < TY, col_sum(ct0.at[pl.ds(32, TX)]), 0.0)
            start_stage1(1, t, cells_out(cur_cols, spread))

        start_halo(t)

        of_stage1(0, t).wait_recv()
        start_stage2(0, t, rows_result(0, t))

        @pl.when(t < ITERS)
        def _():
            of_stage1(1, t).wait_recv()
            start_stage2(1, t, rows_result(1, t))

        of_halo(t).wait_recv()
        assemble(t, own[0:TX, :])
        for k in range(8):
            xa[:, 256 * k:256 * k + 128] = et0[k + 2:k + 2 + AIN, :].astype(BF16)
            xa[:, 256 * k + 128:256 * k + 256] = et1[k + 2:k + 2 + AIN, :].astype(BF16)
        for group in range(8):
            piece = dot(xa[...], wa[group])
            lo = 8 * group
            if group == 0:
                at0[...] = piece[lo:lo + AOUT, 0:128]
                at1[...] = piece[lo:lo + AOUT, 128:256]
            else:
                at0[...] += piece[lo:lo + AOUT, 0:128]
                at1[...] += piece[lo:lo + AOUT, 128:256]

        of_stage2(0, t).wait_recv()
        turned = turned_sums(t)
        out = dot_cols(turned[0:16], ts, 0, 256)
        for u in range(COARSE):
            for ref, first in ((ub0, 0), (ub1, 128)):
                ref[pl.ds(6 + u, 8, stride=COARSE), :] = out[0:8, first:first + 128]
                ref[pl.ds(206 + u, 8, stride=COARSE), :] = out[8:16, first:first + 128]
        new0 = ct0[0:AOUT, :] - STEP * (at0[...] + ADJ_SCALE * ub0[24:24 + AOUT, :])
        new1 = ct1[0:AOUT, :] - STEP * (at1[...] + ADJ_SCALE * ub1[24:24 + AOUT, :])
        both_ref[TX:, :] = new0[32:32 + TX, 0:TY]
        ct0[0:AOUT, :] = new0.astype(BF16).astype(F32) * (row_ok * mask0)
        ct1[0:AOUT, :] = new1.astype(BF16).astype(F32) * (row_ok * mask1)

        @pl.when(t < ITERS)
        def _():
            blur()
            from_sums = dot_cols(turned[16:24], ts, 256, 384)
            of_stage2(1, t).wait_recv()
            set_back(t, from_sums)
            of_stage1(1, t).wait_send()
            of_stage2(1, t).wait_send()

        of_stage1(0, t).wait_send()
        of_stage2(0, t).wait_send()
        of_halo(t).wait_send()
        return carry

    lax.fori_loop(1, PHASES, iteration, 0)
    put_dose.start()
    put_resist.wait()
    put_dose.wait()


def solution(mesh):
    ns, nn = mesh.shape["stripe"], mesh.shape["scan"]

    def per_device(dose, target, psf):
        held = pl.BlockSpec(memory_space=pl.ANY)
        f = lambda *shape: pltpu.VMEM(shape, F32)
        h = lambda *shape: pltpu.VMEM(shape, BF16)
        both = pl.pallas_call(
            lambda *refs: kernel(ns, nn, *refs),
            out_shape=jax.ShapeDtypeStruct((2 * TX, TY), F32),
            in_specs=[held] * 3,
            out_specs=held,
            scratch_shapes=[
                h(TX, TY), pltpu.VMEM((TX, TY), jnp.int32), h(TAPS, TAPS), f(2 * TX, TY),
                f(PHASES, 2 * ns, 4, 128), f(PHASES, 2 * ns, 8, 128),
                f(PHASES, nn // 2, 2, 128), f(PHASES, nn // 2, 4, 128), h(PHASES, HALO, 128),
                h(HALO, 128),
                f(EROWS, 128), f(EROWS, 128), f(CROWS, 128), f(CROWS, 128),
                f(AOUT, 128), f(AOUT, 128),
                h(8, 2048, 256), h(4, 2048, 256), h(80, 3200),
                f(64, 128), f(64, 128), f(64, 128), f(128, 128),
                h(AIN, 2048), h(BIN, 2048),
                f(232, 128), f(232, 128), f(40, 128), f(16, 128),
                h(128, 512), h(3, nn * 4, 384), h(3, nn * 8, 128), f(448, 128), f(448, 128), f(232, 128), f(TX, 128),
                pltpu.SemaphoreType.DMA((5,)), pltpu.SemaphoreType.DMA((PHASES, 5)),
                pltpu.SemaphoreType.DMA((5,)),
            ],
            compiler_params=pltpu.CompilerParams(
                collective_id=0, has_side_effects=True, vmem_limit_bytes=60 << 20
            ),
            name="dose",
        )(dose, target, psf)
        return both[0:TX], both[TX:]

    return jax.shard_map(
        per_device, mesh=mesh,
        in_specs=(P("stripe", "scan"), P("stripe", "scan"), P()),
        out_specs=(P("stripe", "scan"), P("stripe", "scan")),
        check_vma=False,
    )
```

```python
import math

import jax
import jax.numpy as jnp
from jax import lax
from jax.experimental import pallas as pl
from jax.experimental.pallas import tpu as pltpu
from jax.sharding import PartitionSpec as P

TX, TY = 200, 100
TAPS = 61
COARSE = 25
SIGMA = 40
ITERS = 4
RIM = 30
BACK = 0.6
GAIN = 3.0
LEVEL = 1.5
STEP = 0.5
CROW, CCOL = TX // COARSE, TY // COARSE
ADJ_SCALE = BACK / (COARSE * COARSE)

MESH = pl.DeviceIdType.MESH
F32, BF16 = jnp.float32, jnp.bfloat16
HI = lax.Precision.HIGHEST

EROWS = 336
CROWS = 272
AOUT = 264
AIN = 320
BIN = 256
PHASES = ITERS + 1
SIDE = 112
SIDE_ROWS = 104
CORNER = 32
EDGE = 64
AT = (0, SIDE, 2 * SIDE, 2 * SIDE + CORNER, 2 * SIDE + 2 * CORNER, 2 * SIDE + 3 * CORNER,
      2 * SIDE + 4 * CORNER, 2 * SIDE + 4 * CORNER + EDGE)
HALO = 2 * SIDE + 4 * CORNER + 2 * EDGE


def iota(shape, dim):
    return lax.broadcasted_iota(jnp.int32, shape, dim)


def dot(a, b, precision=None):
    return jnp.dot(a, b, precision=precision, preferred_element_type=F32)


def dot_nt(a, b, precision=None):
    return lax.dot_general(
        a, b, (((1,), (1,)), ((), ())), precision=precision, preferred_element_type=F32
    )


def gauss(dist):
    d = dist.astype(F32)
    return jnp.exp(-d * d / (2.0 * SIGMA * SIGMA)) / (math.sqrt(2.0 * math.pi) * SIGMA)


def cell_of(col):
    out = jnp.full(col.shape, -3, jnp.int32)
    for k in range(-2, 7):
        out = out + jnp.where(col >= COARSE * k, 1, 0)
    return out


def kernel(
    ns, nn, dose_hbm, target_hbm, psf_hbm, both_hbm, dose_ref, target_ref, psf_ref, both_ref,
    gs1, gd1, gs2, gd2, halo, tile, et0, et1, ct0, ct1, at0, at1, wa, wf, vv,
    ps, rf, ra, fr, xa, xb, err, own, zs, sc, mw, ts, td, ub0, ub1, bk, bl, mk,
    send_sem, recv_sem, local_sem,
):
    s = lax.axis_index("stripe")
    n = lax.axis_index("scan")
    ncx, ncy = ns * CROW, nn * CCOL
    up, down = lax.rem(s + ns - 1, ns), lax.rem(s + 1, ns)
    left, right = lax.rem(n + nn - 1, nn), lax.rem(n + 1, nn)

    x_lo = lax.rem(n // 2, 2)
    core = lax.rem(n, 2)
    far = lambda count: sorted(range(count), key=lambda k: -min(k, count - k))
    plane, column = [], []
    for k in far(ns):
        for flip in (1, 0):
            if k or flip:
                plane.append((lax.rem(s + k, ns), n + 2 * flip * (1 - 2 * x_lo)))
    for k in far(nn // 4):
        for flip in (1, 0):
            if k or flip:
                column.append((s, lax.rem(n + 4 * k, nn) + flip * (1 - 2 * core)))
    own1, own2 = x_lo * ns + s, (n // 4) * 2 + core
    barrier = pltpu.get_barrier_semaphore()

    def hello(a, b):
        pl.semaphore_signal(barrier, inc=1, device_id=(a, b), device_id_type=MESH)

    for a in (up, down):
        for b in (left, right):
            hello(a, b)
    for b in (left, right):
        hello(s, b)
    for a, b in plane + column:
        hello(a, b)

    get_dose = pltpu.make_async_copy(dose_hbm, dose_ref, local_sem.at[0])
    get_psf = pltpu.make_async_copy(psf_hbm, psf_ref, local_sem.at[1])
    get_target = pltpu.make_async_copy(target_hbm, target_ref, local_sem.at[2])
    get_dose.start()
    get_psf.start()
    get_target.start()
    put_resist = pltpu.make_async_copy(both_ref.at[pl.ds(0, TX)], both_hbm.at[pl.ds(0, TX)], local_sem.at[3])
    put_dose = pltpu.make_async_copy(both_ref.at[pl.ds(TX, TX)], both_hbm.at[pl.ds(TX, TX)], local_sem.at[4])

    lane = iota((1, 128), 1)

    def fold(value):
        half = value.shape[0] // 2
        return jnp.where(lane < 64, value[0:half], pltpu.roll(value[half:], 64, 1)).astype(BF16)

    def field_out(value):
        last = pltpu.roll(value, 92, 1)
        more = jnp.zeros((2 * SIDE_ROWS - TX, 128), F32)
        tile[AT[0]:AT[0] + SIDE_ROWS, :] = fold(jnp.concatenate([last, more], axis=0))
        tile[AT[1]:AT[1] + SIDE_ROWS, :] = fold(jnp.concatenate([value, more], axis=0))
        tile[AT[2]:AT[2] + CORNER, :] = fold(last[TX - EDGE:])
        tile[AT[3]:AT[3] + CORNER, :] = fold(value[TX - EDGE:])
        tile[AT[4]:AT[4] + CORNER, :] = fold(last[0:EDGE])
        tile[AT[5]:AT[5] + CORNER, :] = fold(value[0:EDGE])
        tile[AT[6]:AT[6] + EDGE, :] = value[TX - EDGE:].astype(BF16)
        tile[AT[7]:AT[7] + EDGE, :] = value[0:EDGE].astype(BF16)

    def col_sum(ref):
        total = ref[pl.ds(0, CROW, stride=COARSE), :]
        for u in range(1, COARSE):
            total = total + ref[pl.ds(u, CROW, stride=COARSE), :]
        return total

    pick_row = iota((8, 128), 0)
    pick_cell = cell_of(iota((8, 128), 1))
    pick_in = iota((8, 128), 1) < TY
    pick_sum = jnp.where((pick_cell == pick_row) & pick_in, 1.0, 0.0)
    pick_dose = jnp.where((pick_cell == pick_row - 2) & pick_in, 1.0, 0.0)
    zs[...] = jnp.zeros_like(zs)
    sc[...] = jnp.zeros_like(sc)

    def sums_out(err_cols):
        parts = []
        for _ in range(3):
            parts.append(err_cols.astype(BF16).astype(F32))
            err_cols = err_cols - parts[-1]
        parts.append(jnp.zeros_like(err_cols))
        picks = jnp.concatenate([pick_sum, jnp.zeros_like(pick_sum)], axis=0).astype(BF16)
        sc[:, 0:32] = dot_nt(picks, jnp.concatenate(parts, axis=0).astype(BF16))
        got = sc[0:8, :]
        got = got + (pltpu.roll(got, 128 - CROW, 1) + pltpu.roll(got, 128 - 2 * CROW, 1))
        return pltpu.roll(jnp.where(lane < CROW, got, 0.0), s * CROW, 1)[0:4]

    def cells_out(cur_cols, spread):
        sc[8:16, 0:8] = dot_nt(pick_dose, cur_cols, HI)
        cells = pltpu.roll(jnp.where(lane < CROW, sc[8:16, :], 0.0), 64 + s * CROW, 1)
        cells = cells * (1.0 / (COARSE * COARSE))
        if spread is not None:
            zs[:, 0:8] = spread
            part = jnp.zeros((8, 128), F32)
            for d in range(5):
                part = part + pltpu.roll(zs[8 * d:8 * d + 8, :], 62 + d + s * CROW, 1)
            cells = cells - (STEP / (COARSE * COARSE)) * part
        return jnp.where(lane < 64, 0.0, cells)

    stage1, stage2 = (gs1, gd1), (gs2, gd2)

    def start_stage1(which, t, value):
        ref = stage1[which].at[t, own1]
        ref[...] = value
        for a, b in plane:
            pltpu.make_async_remote_copy(
                ref, ref, send_sem.at[which], recv_sem.at[t, which],
                device_id=(a, b), device_id_type=MESH,
            ).start()

    def start_stage2(which, t, value):
        ref = stage2[which].at[t, own2]
        ref[...] = value
        for a, b in column:
            pltpu.make_async_remote_copy(
                ref, ref, send_sem.at[2 + which], recv_sem.at[t, 2 + which],
                device_id=(a, b), device_id_type=MESH,
            ).start()

    def start_halo(t):
        sizes = (SIDE, SIDE, CORNER, CORNER, CORNER, CORNER, EDGE, EDGE)
        to = ((s, right), (s, left), (down, right), (down, left), (up, right), (up, left), (down, n), (up, n))
        for k in (2, 3, 4, 5, 6, 7, 0, 1):
            part = pl.ds(AT[k], sizes[k])
            pltpu.make_async_remote_copy(
                tile.at[part], halo.at[t, part], send_sem.at[4], recv_sem.at[t, 4],
                device_id=to[k], device_id_type=MESH,
            ).start()

    def all_of(ref, sem_send, sem_recv):
        return pltpu.make_async_remote_copy(
            ref, ref, sem_send, sem_recv, device_id=(s, right), device_id_type=MESH
        )

    def of_stage1(which, t):
        return all_of(stage1[which].at[t, pl.ds(0, 2 * ns - 1)], send_sem.at[which], recv_sem.at[t, which])

    def of_stage2(which, t):
        return all_of(stage2[which].at[t, pl.ds(0, nn // 2 - 1)], send_sem.at[2 + which], recv_sem.at[t, 2 + which])

    def of_halo(t):
        return all_of(halo.at[t], send_sem.at[4], recv_sem.at[t, 4])

    def assemble(t, centre):
        yes = lambda c: jnp.where(c, 1.0, 0.0).astype(F32)
        has_up, has_down = yes(s > 0), yes(s < ns - 1)
        has_left, has_right = yes(n > 0), yes(n < nn - 1)

        def band(row, rows, mid, lhs, rhs, flag):
            lhs = jnp.concatenate([pltpu.roll(lhs, 64, 1), lhs], axis=0)[0:rows] * (has_left * flag)
            rhs = jnp.concatenate([pltpu.roll(rhs, TY, 1), pltpu.roll(rhs, 36, 1)], axis=0)[0:rows] * (has_right * flag)
            et0[row:row + rows, :] = jnp.where(lane < TY, mid * flag, rhs)
            et1[row:row + rows, :] = jnp.where(lane < 32, rhs, jnp.where(lane >= 68, lhs, 0.0))

        def part(k, rows):
            return halo[t, pl.ds(AT[k], rows), :].astype(F32)

        band(0, EDGE, part(6, EDGE), part(2, CORNER), part(3, CORNER), has_up)
        band(EDGE, TX, centre, part(0, SIDE_ROWS), part(1, SIDE_ROWS), jnp.float32(1.0))
        band(EDGE + TX, EDGE, part(7, EDGE), part(4, CORNER), part(5, CORNER), has_down)

    def rows_result(which, t):
        totals = []
        for x in range(2):
            total = stage1[which][t, x * ns]
            for k in range(1, ns):
                total = total + stage1[which][t, x * ns + k]
            totals.append(total)
        total = jnp.concatenate(totals, axis=0)
        rows = total.shape[0]
        parts = []
        for _ in range(3):
            parts.append(total.astype(BF16).astype(F32))
            total = total - parts[-1]
        p = dot(jnp.concatenate(parts, axis=0).astype(BF16), mw[...])
        out = p[2 * rows:3 * rows, 0:128] + p[rows:2 * rows, 128:256] + p[0:rows, 256:384]
        out = out + p[rows:2 * rows, 0:128] + p[0:rows, 128:256]
        out = out + p[0:rows, 0:128]
        row = iota((rows, 128), 0)
        out = jnp.where(jnp.bitwise_and(row, 3) == iota((rows, 128), 1) // 32, out, 0.0)
        return jnp.concatenate(
            [jnp.sum(out[4 * k:4 * k + 4], axis=0, keepdims=True) for k in range(rows // 4)], axis=0)

    def turned_sums(t):
        stack = jnp.concatenate([gs2[t].reshape(nn, 128), jnp.zeros((128 - nn, 128), F32)], axis=0)
        turned = jnp.transpose(stack)
        out = turned[0:32]
        for k in range(1, 4):
            out = out + pltpu.roll(turned[32 * k:32 * k + 32], 32 * k, 1)
        return out

    def turned_cells(t):
        stack = jnp.concatenate([gd2[t].reshape(nn * 2, 128), jnp.zeros((64, 128), F32)], axis=0)
        turned = jnp.transpose(stack)
        return jnp.concatenate(
            [turned[0:32] + pltpu.roll(turned[32:64], 64, 1), turned[64:96] + pltpu.roll(turned[96:128], 64, 1)],
            axis=1)

    def dot_cols(lhs, table, first, last):
        rows = lhs.shape[0]
        parts = []
        for _ in range(3):
            parts.append(lhs.astype(BF16).astype(F32))
            lhs = lhs - parts[-1]
        p = dot(jnp.concatenate(parts, axis=0).astype(BF16), table[0, :, first:last])
        q2 = dot(jnp.concatenate(parts[0:2], axis=0).astype(BF16), table[1, :, first:last])
        q3 = dot(parts[0].astype(BF16), table[2, :, first:last])
        out = p[2 * rows:] + q2[rows:] + q3
        out = out + p[rows:2 * rows] + q2[0:rows]
        return out + p[0:rows]

    def set_back(t, from_sums):
        value = dot_cols(turned_cells(t)[24:32], td, 0, 128)
        value = BACK * (value if from_sums is None else value + from_sums)
        for u in range(COARSE):
            bk[pl.ds(u, CROW, stride=COARSE), :] = value

    def blur():
        for k in range(8):
            xb[:, 256 * k:256 * k + 128] = ct0[k + 2:k + 2 + BIN, :].astype(BF16)
            xb[:, 256 * k + 128:256 * k + 256] = ct1[k + 2:k + 2 + BIN, :].astype(BF16)
        blurred = None
        for pair in range(4):
            piece = dot(xb[...], wf[pair])
            lo = 16 * pair
            both = piece[lo:lo + TX, 0:128] + piece[lo + 8:lo + 8 + TX, 128:256]
            blurred = both if blurred is None else blurred + both
        bl[...] = blurred

    get_dose.wait()
    dose = jnp.zeros((TX, 128), F32)
    own[0:TX, :] = dose
    own[0:TX, 0:TY] = dose_ref[...].astype(F32)
    tile[...] = jnp.zeros_like(tile)
    field_out(own[0:TX, :])
    first_payload = cells_out(col_sum(own), None)

    ps[...] = jnp.zeros_like(ps)
    get_psf.wait()
    ps[0:TAPS, 0:TAPS] = psf_ref[...].astype(F32)
    taps = ps[...]
    taps_h = taps.astype(BF16)
    b_at, l_at = iota((128, 128), 0), iota((128, 128), 1)
    perm_f = jnp.where((l_at == lax.rem(RIM - b_at + 256, 128)) & (b_at < TAPS), 1.0, 0.0).astype(BF16)
    perm_a = jnp.where((l_at == lax.rem(b_at - RIM + 256, 128)) & (b_at < TAPS), 1.0, 0.0).astype(BF16)
    flip = jnp.where(iota((64, 64), 1) == TAPS - 1 - iota((64, 64), 0), 1.0, 0.0).astype(BF16)
    rf[...] = dot(taps_h, perm_f)
    ra[...] = dot(dot(flip, taps_h).astype(BF16), perm_a)

    g_row = jnp.bitwise_and(b_at, 63)
    l32 = jnp.bitwise_and(l_at, 31)
    full_rows = gauss(iota((ncx, ncx), 0) - iota((ncx, ncx), 1))
    l64 = jnp.bitwise_and(iota((ncx, 128), 1), 31)
    twice = dot(full_rows, gauss(iota((ncx, 128), 0) - (s * CROW + l64 - 16)), HI)
    upper = jnp.concatenate([twice, jnp.zeros((128 - ncx, 128), F32)], axis=0)
    low = b_at < 64
    table = jnp.where(low & (l32 < 12), gauss(g_row - (s * CROW + l32 - 2)), 0.0)
    table = table + jnp.where(low & (l32 >= 16) & (l32 < 24), upper, 0.0)
    table = table + jnp.where((~low) & (l32 >= 24), gauss(g_row - (s * CROW + l32 - 24)), 0.0)
    table = jnp.where(g_row < ncx, table, 0.0)
    for k in range(3):
        rounded = table.astype(BF16)
        mw[:, 128 * k:128 * k + 128] = rounded
        table = table - rounded.astype(F32)
    mw[:, 384:512] = jnp.zeros((128, 128), BF16)

    k_at, a_at = iota((128, 64), 0), iota((128, 64), 1)
    u_at = k_at // 5
    low_a = COARSE * (k_at - 5 * u_at - 2) - u_at + RIM
    rows_w = jnp.where((a_at >= low_a) & (a_at < low_a + COARSE), 1.0, 0.0).astype(BF16)
    x_at = -2 * COARSE - jnp.where(l_at < 16, l_at, l_at - 128)
    cols_w = jnp.where((b_at >= x_at + RIM) & (b_at < x_at + RIM + COARSE), 1.0, 0.0)
    fr[...] = dot(dot(rows_w, taps_h), cols_w, HI)
    j8 = iota((8, 128), 0)
    c8 = iota((8, 128), 1)
    xx = COARSE * (j8 - 2) - c8
    inside = (xx >= RIM - 84) & (xx <= RIM) & (c8 < TY)
    for u in range(COARSE):
        pieces = []
        for d in range(5):
            row = jnp.broadcast_to(fr[5 * u + d:5 * u + d + 1, :], (8, 128))
            row = pltpu.roll(pltpu.roll(row, 0, 1, stride=12, stride_axis=0), 0, 1, stride=13, stride_axis=0)
            pieces.append(jnp.where(inside, row, 0.0))
        for d in range(5):
            top = pieces[d].astype(BF16).astype(F32)
            both = jnp.concatenate([top, pieces[d] - top], axis=0).astype(BF16)
            vv[16 * d:16 * d + 16, 128 * u:128 * u + 128] = both

    pl.semaphore_wait(barrier, len(plane) + len(column) + 6)
    start_stage1(1, 0, first_payload)
    start_halo(0)

    near = jnp.abs(b_at - l_at) <= RIM

    def circulant(row):
        full = pltpu.roll(jnp.broadcast_to(row, (128, 128)), 0, 1, stride=1, stride_axis=0)
        return jnp.where(near, full, 0.0).astype(BF16), jnp.where(near, 0.0, full).astype(BF16)

    def one_pair(k, carry):
        pair, shift = k // 8, lax.rem(k, 8)
        at_row = pl.multiple_of(shift * 256, 256)
        for half in range(2):
            tap = pair * 16 + half * 8 + shift
            same, other = circulant(rf[pl.ds(tap, 1), :])
            wf[pair, pl.ds(at_row, 128), half * 128:half * 128 + 128] = same
            wf[pair, pl.ds(at_row + 128, 128), half * 128:half * 128 + 128] = other
            same, other = circulant(ra[pl.ds(tap, 1), :])
            group = pair * 2 + half
            wa[group, pl.ds(at_row, 128), 0:128] = same
            wa[group, pl.ds(at_row, 128), 128:256] = other
            wa[group, pl.ds(at_row + 128, 128), 0:128] = other
            wa[group, pl.ds(at_row + 128, 128), 128:256] = same
        return carry

    lax.fori_loop(0, 32, one_pair, 0)

    of_stage1(1, 0).wait_recv()
    start_stage2(1, 0, rows_result(1, 0))

    def split(table, first, value):
        for k in range(3):
            rounded = value.astype(BF16)
            table[k, :, first:first + value.shape[1]] = rounded
            value = value - rounded.astype(F32)

    def sum_col(width):
        at = iota((nn * 4, width), 0)
        z, c, x = jnp.bitwise_and(at, 31) // 4, jnp.bitwise_and(at // 2, 1), jnp.bitwise_and(at, 1)
        return CCOL * (4 * z + 2 * x + c) + at // 32

    pos = iota((nn * 4, 256), 1)
    col = jnp.where(pos < 160, pos, pos - 256)
    split(ts, 0, gauss(sum_col(256) - (CCOL * n + cell_of(col))))
    mid = gauss(iota((ncy, 128), 0) - (CCOL * n + cell_of(iota((ncy, 128), 1))))
    outer = gauss(sum_col(ncy) - iota((nn * 4, ncy), 1))
    split(ts, 256, (-STEP * ADJ_SCALE) * dot(outer, mid, HI))
    at = iota((nn * 8, 128), 0)
    pos = jnp.bitwise_and(at, 63)
    z, c, x = pos // 8, jnp.bitwise_and(pos // 4, 1), jnp.bitwise_and(pos // 2, 1)
    at = CCOL * (4 * z + 2 * x + c) + 4 * jnp.bitwise_and(at, 1) + at // 64 - 2
    lane_cell = CCOL * n + cell_of(iota((nn * 8, 128), 1))
    split(td, 0, jnp.where((at >= 0) & (at < ncy), gauss(at - lane_cell), 0.0))


    et0[AIN + 8:, :] = jnp.zeros((EROWS - AIN - 8, 128), F32)
    et1[AIN + 8:, :] = jnp.zeros((EROWS - AIN - 8, 128), F32)
    ct0[AOUT:, :] = jnp.zeros((CROWS - AOUT, 128), F32)
    ct1[AOUT:, :] = jnp.zeros((CROWS - AOUT, 128), F32)

    of_halo(0).wait_recv()
    assemble(0, own[0:TX, :])
    ct0[0:AOUT, :] = et0[32:32 + AOUT, :]
    ct1[0:AOUT, :] = et1[32:32 + AOUT, :]

    blur()
    of_stage2(1, 0).wait_recv()
    set_back(0, None)
    of_stage1(1, 0).wait_send()
    of_stage2(1, 0).wait_send()
    of_halo(0).wait_send()

    yes = lambda c: jnp.where(c, 1.0, 0.0).astype(F32)
    row_ok = jnp.ones((AOUT, 1), F32)
    r_at = iota((AOUT, 1), 0) - 32
    row_ok = jnp.where(r_at < 0, yes(s > 0), jnp.where(r_at >= TX, yes(s < ns - 1), 1.0))
    mask0 = jnp.where(lane < TY, 1.0, yes(n < nn - 1))
    mask1 = jnp.where(lane < 32, yes(n < nn - 1), yes(n > 0))

    get_target.wait()
    mk[...] = jnp.zeros_like(mk)
    mk[:, 0:TY] = target_ref[...].astype(F32)

    def iteration(t, carry):
        exposure = bl[...] + bk[0:TX, :]
        resist = jax.nn.sigmoid(GAIN * (exposure - LEVEL))
        error = (resist - mk[...]) * GAIN * resist * (1.0 - resist)
        error = jnp.where(lane < TY, error, 0.0)
        err[0:TX, :] = error
        start_stage1(0, t, sums_out(col_sum(err)))
        half = error.astype(BF16).astype(F32)
        own[0:TX, :] = half
        field_out(half)
        start_halo(t)
        both_ref[0:TX, :] = resist[:, 0:TY]

        @pl.when(t == ITERS)
        def _():
            put_resist.start()
        @pl.when(t < ITERS)
        def _():
            cells_in = jnp.concatenate(
                [own[pl.ds(u, CROW, stride=COARSE), :].astype(BF16) for u in range(COARSE)], axis=1)
            two = dot_nt(vv[...], cells_in)
            spread = jnp.concatenate([two[16 * d:16 * d + 8] + two[16 * d + 8:16 * d + 16] for d in range(5)], axis=0)
            cur_cols = jnp.where(lane < TY, col_sum(ct0.at[pl.ds(32, TX)]), 0.0)
            start_stage1(1, t, cells_out(cur_cols, spread))


        of_stage1(0, t).wait_recv()
        start_stage2(0, t, rows_result(0, t))

        @pl.when(t < ITERS)
        def _():
            of_stage1(1, t).wait_recv()
            start_stage2(1, t, rows_result(1, t))

        of_halo(t).wait_recv()
        assemble(t, own[0:TX, :])
        for k in range(8):
            xa[:, 256 * k:256 * k + 128] = et0[k + 2:k + 2 + AIN, :].astype(BF16)
            xa[:, 256 * k + 128:256 * k + 256] = et1[k + 2:k + 2 + AIN, :].astype(BF16)
        for group in range(8):
            piece = dot(xa[...], wa[group])
            lo = 8 * group
            if group == 0:
                at0[...] = piece[lo:lo + AOUT, 0:128]
                at1[...] = piece[lo:lo + AOUT, 128:256]
            else:
                at0[...] += piece[lo:lo + AOUT, 0:128]
                at1[...] += piece[lo:lo + AOUT, 128:256]

        of_stage2(0, t).wait_recv()
        turned = turned_sums(t)
        out = dot_cols(turned[0:16], ts, 0, 256)
        for u in range(COARSE):
            for ref, first in ((ub0, 0), (ub1, 128)):
                ref[pl.ds(6 + u, 8, stride=COARSE), :] = out[0:8, first:first + 128]
                ref[pl.ds(206 + u, 8, stride=COARSE), :] = out[8:16, first:first + 128]
        new0 = ct0[0:AOUT, :] - STEP * (at0[...] + ADJ_SCALE * ub0[24:24 + AOUT, :])
        new1 = ct1[0:AOUT, :] - STEP * (at1[...] + ADJ_SCALE * ub1[24:24 + AOUT, :])
        both_ref[TX:, :] = new0[32:32 + TX, 0:TY]
        ct0[0:AOUT, :] = new0.astype(BF16).astype(F32) * (row_ok * mask0)
        ct1[0:AOUT, :] = new1.astype(BF16).astype(F32) * (row_ok * mask1)

        @pl.when(t < ITERS)
        def _():
            blur()
            from_sums = dot_cols(turned[16:24], ts, 256, 384)
            of_stage2(1, t).wait_recv()
            set_back(t, from_sums)
            of_stage1(1, t).wait_send()
            of_stage2(1, t).wait_send()

        of_stage1(0, t).wait_send()
        of_stage2(0, t).wait_send()
        of_halo(t).wait_send()
        return carry

    lax.fori_loop(1, PHASES, iteration, 0)
    put_dose.start()
    put_resist.wait()
    put_dose.wait()


def solution(mesh):
    ns, nn = mesh.shape["stripe"], mesh.shape["scan"]

    def per_device(dose, target, psf):
        held = pl.BlockSpec(memory_space=pl.ANY)
        f = lambda *shape: pltpu.VMEM(shape, F32)
        h = lambda *shape: pltpu.VMEM(shape, BF16)
        both = pl.pallas_call(
            lambda *refs: kernel(ns, nn, *refs),
            out_shape=jax.ShapeDtypeStruct((2 * TX, TY), F32),
            in_specs=[held] * 3,
            out_specs=held,
            scratch_shapes=[
                h(TX, TY), pltpu.VMEM((TX, TY), jnp.int32), h(TAPS, TAPS), f(2 * TX, TY),
                f(PHASES, 2 * ns, 4, 128), f(PHASES, 2 * ns, 8, 128),
                f(PHASES, nn // 2, 2, 128), f(PHASES, nn // 2, 4, 128), h(PHASES, HALO, 128),
                h(HALO, 128),
                f(EROWS, 128), f(EROWS, 128), f(CROWS, 128), f(CROWS, 128),
                f(AOUT, 128), f(AOUT, 128),
                h(8, 2048, 256), h(4, 2048, 256), h(80, 3200),
                f(64, 128), f(64, 128), f(64, 128), f(128, 128),
                h(AIN, 2048), h(BIN, 2048),
                f(232, 128), f(232, 128), f(40, 128), f(16, 128),
                h(128, 512), h(3, nn * 4, 384), h(3, nn * 8, 128), f(448, 128), f(448, 128), f(232, 128), f(TX, 128), f(TX, 128),
                pltpu.SemaphoreType.DMA((5,)), pltpu.SemaphoreType.DMA((PHASES, 5)),
                pltpu.SemaphoreType.DMA((5,)),
            ],
            compiler_params=pltpu.CompilerParams(
                collective_id=0, has_side_effects=True, vmem_limit_bytes=60 << 20
            ),
            name="dose",
        )(dose, target, psf)
        return both[0:TX], both[TX:]

    return jax.shard_map(
        per_device, mesh=mesh,
        in_specs=(P("stripe", "scan"), P("stripe", "scan"), P()),
        out_specs=(P("stripe", "scan"), P("stripe", "scan")),
        check_vma=False,
    )
```
